32 devices in a mesh: tgt: 8 (over z, core), sup: 4 (over y, x).
Axes of the slice: x: 2, y: 2, z: 4, core: 2. Of those that a mesh axis runs over, the one named last changes fastest.
Arguments:
- target_pool: float32 [512, 3, 1024], P('tgt'), may hold values from -6 to 6
- target_index: int32 [64], P('tgt'), may hold values from 0 to 511, as said below
- target_labels: int32 [64], P('tgt'), may hold values from 0 to 99
- dual_weights: float32 [128, 100], P('sup'), may hold values from -0.5 to 0.5
- support_images: float32 [128, 3, 1024], P(('sup', 'tgt')), may hold values from -6 to 6
Outputs:
- residual: float32 [64, 100], P('tgt')
- support_grad: float32 [128, 3, 1024], P(('sup', 'tgt'))
The draws below stay inside these ranges and needn't reach their ends.
Inputs may be any that keep to these rules, and one draw needn't show every extreme that they name: `target_index`: for each j, the targets 8 * j to 8 * (j + 1) - 1 name distinct candidates among 64 * j to 64 * (j + 1) - 1.
All inputs are finite; a program needn't handle non-finite values.
Results may differ from the reference program's by a relative error of at most 0.0003.
Values sent between devices are 32-bit elements; how exact they have to be, the bound alone decides.
A program may use at most 64 MiB of HBM per device.

```python
import math
import jax
import jax.numpy as jnp
from jax import lax

CHANNELS = 3
SIDE = 32
CLASSES = 100
LAYERS = 3
TGT_DEV = 8
POOL_DEV = 64
PIXELS = 1024
TARGETS = 64
SUPPORT = 128
POOL = 512


def draw_target_index(key, part):
    blocks = TARGETS // TGT_DEV
    block_keys = jax.random.split(key, blocks)
    block_ids = jnp.arange(blocks)

    def one_block(block_key, block_id):
        first_key, second_key, third_key = jax.random.split(block_key, 3)
        drawn = jax.random.permutation(first_key, POOL_DEV)[:TGT_DEV]
        others = jax.random.permutation(second_key, POOL_DEV - 1)[:TGT_DEV - 1]
        with_low = jnp.concatenate([others + 1, jnp.zeros((1,), jnp.int32)])
        with_high = jnp.concatenate([others, jnp.full((1,), POOL_DEV - 1, jnp.int32)])
        picked = jnp.where(block_id == 0, with_low, jnp.where(block_id == blocks - 1, with_high, drawn.astype(jnp.int32)))
        order = jax.random.permutation(third_key, TGT_DEV)
        return jnp.take(picked, order)
    chosen = jax.vmap(one_block)(block_keys, block_ids)
    offsets = (block_ids * POOL_DEV)[:, None]
    return (chosen + offsets).reshape(-1).astype(jnp.int32)


def place_ends(array, own_key, low, high):
    index_at = [jax.random.randint(jax.random.fold_in(own_key, axis), (), 0, length) for axis, length in enumerate(array.shape)]
    longest = array.shape.index(max(array.shape))
    beside = index_at[:longest] + [(index_at[longest] + 1) % array.shape[longest]] + index_at[longest + 1:]
    return array.at[tuple(index_at)].set(low).at[tuple(beside)].set(high)


def block_scale(rng, shape, cuts, least, top_value):
    def one(axis_at, blocks):
        steps = jax.random.uniform(jax.random.fold_in(jax.random.fold_in(rng, 6), axis_at), (blocks,), jnp.float32, least / len(cuts), top_value / len(cuts))
        return jnp.repeat(jnp.exp(steps), shape[axis_at] // blocks).reshape((-1,) + (1,) * (len(shape) - axis_at - 1))

    gain = one(*cuts[0])
    for cut in cuts[1:]:
        gain = gain * one(*cut)
    return gain


def noise(key, dims, width, bound, pieces=(), kind=jnp.bfloat16):
    values = jax.random.normal(key, dims, jnp.float32) * width
    if len(pieces) > 0:
        values = block_scale(key, dims, pieces, -0.22, 0.18) * values
    return jnp.clip(values, min=-bound, max=bound).astype(kind)


def setup_inputs(seed: int = 0) -> dict:
    seeds = jax.random.split(jax.random.key(seed), 6)
    target_pool = noise(seeds[0], (POOL, CHANNELS, PIXELS), 1.0, 6.0, ((0, 8),), jnp.float32)
    target_index = draw_target_index(jax.random.fold_in(seeds[5], 71), 0)
    target_labels = place_ends(jax.random.randint(seeds[2], (TARGETS,), 0, CLASSES), jax.random.fold_in(seeds[2], 1), 0, CLASSES - 1).astype(jnp.int32)
    dual_weights = noise(seeds[3], (SUPPORT, CLASSES), SUPPORT ** -0.5, 0.5, ((0, 4),), jnp.float32)
    support_images = noise(seeds[4], (SUPPORT, CHANNELS, PIXELS), 1.0, 6.0, ((0, 32),), jnp.float32)
    return {"target_pool": target_pool, "target_index": target_index, "target_labels": target_labels, "dual_weights": dual_weights, "support_images": support_images}


bias_variance = 0.01

def box_filter(pixel_map):
    column = jnp.arange(PIXELS) % SIDE
    zero_column = jnp.zeros(pixel_map.shape[:-1] + (1,), pixel_map.dtype)
    shifted_right = jnp.concatenate([zero_column, pixel_map[..., :-1]], axis=-1)
    shifted_left = jnp.concatenate([pixel_map[..., 1:], zero_column], axis=-1)
    across = pixel_map + jnp.where(column > 0, shifted_right, 0.0) + jnp.where(column < SIDE - 1, shifted_left, 0.0)
    zero_row = jnp.zeros(pixel_map.shape[:-1] + (SIDE,), pixel_map.dtype)
    shifted_down = jnp.concatenate([zero_row, across[..., :-SIDE]], axis=-1)
    shifted_up = jnp.concatenate([across[..., SIDE:], zero_row], axis=-1)
    return (across + shifted_down + shifted_up) / 9.0

def self_maps(images):
    energy = images[:, 0] * images[:, 0]
    for channel in range(1, CHANNELS):
        energy = energy + images[:, channel] * images[:, channel]
    current = box_filter(energy / CHANNELS) + bias_variance
    levels = [current]
    for layer_index in range(1, LAYERS):
        current = box_filter(current) + bias_variance
        levels.append(current)
    return levels

def rectified(cross, target_level, support_level):
    spread = jnp.sqrt(target_level * support_level - cross * cross)
    polar_angle = jnp.arctan2(spread, cross)
    return ((spread + (math.pi - polar_angle) * cross) / math.pi, spread, polar_angle)

def cross_forward(targets, support, target_levels, support_levels):
    inner_sum = targets[:, None, 0] * support[None, :, 0]
    for channel in range(1, CHANNELS):
        inner_sum = inner_sum + targets[:, None, channel] * support[None, :, channel]
    cross = box_filter(inner_sum / CHANNELS) + bias_variance
    saved_maps = []
    output_map = cross
    for layer_index in range(LAYERS):
        output_map, spread, polar_angle = rectified(cross, target_levels[layer_index][:, None], support_levels[layer_index][None])
        saved_maps.append((spread, polar_angle))
        if layer_index + 1 < LAYERS:
            cross = box_filter(output_map) + bias_variance
    return (lax.optimization_barrier(jnp.mean(output_map, axis=-1)), saved_maps)

def cross_backward(weight, saved_maps, targets, support, support_levels):
    upstream = weight[:, :, None]
    level_grad = None
    for layer_index in range(LAYERS - 1, -1, -1):
        spread, polar_angle = saved_maps[layer_index]
        level_term = lax.optimization_barrier(jnp.sum(upstream * spread, axis=0)) / (2.0 * math.pi * support_levels[layer_index])
        level_grad = level_term if level_grad is None else level_term + box_filter(level_grad)
        upstream = box_filter(upstream * (math.pi - polar_angle) / math.pi)
    energy_grad = box_filter(level_grad) / CHANNELS
    channel_grads = []
    for channel in range(CHANNELS):
        carried = lax.optimization_barrier(jnp.sum(upstream * targets[:, None, channel], axis=0)) / CHANNELS
        channel_grads.append(carried + 2.0 * support[:, channel] * energy_grad)
    return jnp.stack(channel_grads, axis=1)

def reference(target_pool, target_index, target_labels, dual_weights, support_images):
    targets = jnp.take(target_pool, target_index, axis=0)
    onehot = (target_labels[:, None] == jnp.arange(CLASSES)[None, :]).astype(jnp.float32)
    support_levels = self_maps(support_images)
    blocks = targets.reshape((TARGETS // TGT_DEV, TGT_DEV) + targets.shape[1:])

    def block_kernel(block):
        kernel_rows, saved_maps = cross_forward(block, support_images, self_maps(block), support_levels)
        return kernel_rows
    kernel = lax.map(block_kernel, blocks).reshape(TARGETS, SUPPORT)
    predicted = jnp.dot(kernel, dual_weights, precision=lax.Precision.HIGHEST, preferred_element_type=jnp.float32)
    residual = predicted - onehot
    weight = jnp.dot(residual, dual_weights.T, precision=lax.Precision.HIGHEST, preferred_element_type=jnp.float32)
    weight_blocks = weight.reshape(TARGETS // TGT_DEV, TGT_DEV, SUPPORT)

    def block_grad(total, pair_block):
        block, block_weight = pair_block
        kernel_rows, saved_maps = cross_forward(block, support_images, self_maps(block), support_levels)
        return (total + cross_backward(block_weight, saved_maps, block, support_images, support_levels), None)
    support_grad, unused = lax.scan(block_grad, jnp.zeros(support_images.shape, jnp.float32), (blocks, weight_blocks))
    return (residual, support_grad)
```

```python
import functools
import math

import jax
import jax.numpy as jnp
from jax import lax
from jax.experimental import pallas as pl
from jax.experimental.pallas import tpu as pltpu
from jax.sharding import PartitionSpec as P

CHANNELS = 3
SIDE = 32
CLASSES = 100
LAYERS = 3
PIXELS = 1024
BETA = 0.01
PACK = 4
SUB = 8
LANES = 128
MESH = pl.DeviceIdType.MESH
HIGH = lax.Precision.HIGHEST
ACOS = (
    1.5707956895,
    -0.2145428158,
    0.0881710453,
    -0.0459272047,
    0.0206200335,
    -0.0049111629,
)


def masks():
    lane = lax.broadcasted_iota(jnp.int32, (SUB, LANES), 1)
    row = lax.broadcasted_iota(jnp.int32, (SUB, LANES), 0)
    column = lane % SIDE
    return (column > 0, column < SIDE - 1, row > 0, row < SUB - 1, lane // SIDE)


def box_sum(maps, mask):
    right, left, down, up, _ = mask
    axis = maps[0].ndim - 1

    def across(v):
        return (
            v
            + jnp.where(right, pltpu.roll(v, 1, axis), 0.0)
            + jnp.where(left, pltpu.roll(v, LANES - 1, axis), 0.0)
        )

    before = jnp.where(down, pltpu.roll(maps[3], 1, axis - 1), 0.0)
    after = jnp.where(up, pltpu.roll(maps[0], SUB - 1, axis - 1), 0.0)
    low = maps[0] + maps[1]
    high = maps[2] + maps[3]
    return [across(v) for v in (before + low, low + maps[2], maps[1] + high, high + after)]


def interleave(images, mask):
    group = mask[4]
    out = []
    for k in range(PACK):
        total = None
        for m in range(PACK):
            shift = ((m - k) * SIDE) % LANES
            moved = images[m] if shift == 0 else pltpu.roll(images[m], shift, 1)
            total = moved if total is None else jnp.where(group == m, moved, total)
        out.append(total)
    return out


def replicate(image, mask):
    group = mask[4]
    out = []
    rolled = [image] + [pltpu.roll(image, SIDE * s, 1) for s in range(1, PACK)]
    for k in range(PACK):
        total = None
        for m in range(PACK):
            moved = rolled[(m - k) % PACK]
            total = moved if total is None else jnp.where(group == m, moved, total)
        out.append(total)
    return out


def levels_of(images, mask):
    energy = []
    for k in range(PACK):
        total = images[0][k] * images[0][k]
        for channel in range(1, CHANNELS):
            total = total + images[channel][k] * images[channel][k]
        energy.append(total * (1.0 / CHANNELS))
    levels = []
    current = energy
    for _ in range(LAYERS):
        current = [v * (1.0 / 9.0) + BETA for v in box_sum(current, mask)]
        levels.append(current)
    return levels


def split_rows(v):
    high = v.astype(jnp.bfloat16)
    rest = v - high.astype(jnp.float32)
    middle = rest.astype(jnp.bfloat16)
    low = (rest - middle.astype(jnp.float32)).astype(jnp.bfloat16)
    return jnp.concatenate([high, middle, low], axis=1)


def fold(a, b, keep, shift):
    return jnp.where(keep, a, b) + pltpu.roll(jnp.where(keep, b, a), shift, a.ndim - 1)


def kernel(
    nt, ns, own_t, own_s,
    index_hbm, label_hbm, pool_hbm, dual_hbm, support_hbm,
    residual_ref, grad_ref,
    index_ref, label_ref, pool_a, pool_b, pool_c, support_ref,
    tbuf, dbuf, lbuf, kbuf, srep, sroot, shalf, tlev, mid, held, amp, ang, unit, ksum, wexp, pred, flat,
    in_sem, plane_send, plane_recv, swap_send, part_send, part_recv,
    dual_send, dual_recv, label_send, label_recv, k_send, k_recv,
):
    ti = lax.axis_index("tgt")
    si = lax.axis_index("sup")
    pool_refs = (pool_a, pool_b, pool_c)
    chips = nt // 2
    chip = ti // 2
    core = ti % 2
    ndev = nt * ns
    me = si * nt + ti
    groups_own = own_t // PACK
    groups = nt * groups_own
    targets = nt * own_t
    mask = masks()
    share = 2 if groups_own % 2 == 0 and ns % 2 == 0 else 1
    beside = si + 1 - 2 * (si % 2)
    carried = [r * share + si % share for r in range(groups_own // share)]
    swapped = [r * share + (si + 1) % share for r in range(groups_own // share)] if share == 2 else []

    barrier = pltpu.get_barrier_semaphore()

    def others(action):
        for s in range(ns):
            for t in range(nt):
                pl.when((si != s) | (ti != t))(functools.partial(action, t, s))

    def greet(t, s):
        pl.semaphore_signal(barrier, inc=1, device_id=(t, s), device_id_type=MESH)

    for step in range(1, ns):
        greet(ti, lax.rem(si + step, ns))
    greet(chip * 2 + 1 - core, si)
    pl.when(chip > 0)(lambda: greet(ti - 2, si))
    pl.when(chip < chips - 1)(lambda: greet(ti + 2, si))

    def fetch(at, src, dst):
        return pltpu.make_async_copy(src, dst, in_sem.at[at])

    loads = [
        fetch(0, index_hbm, index_ref),
        fetch(1, label_hbm, label_ref),
        fetch(2, dual_hbm, dbuf.at[si]),
        fetch(3, support_hbm, support_ref),
    ] + [fetch(4 + c, pool_hbm.at[c], pool_refs[c]) for c in range(CHANNELS)]
    for at in (0, 4, 5, 6, 3, 2, 1):
        loads[at].start()

    def plane_copy(source_chip, gl, target_chip):
        part = tbuf.at[source_chip * 2 + core, gl]
        return pltpu.make_async_remote_copy(
            src_ref=part,
            dst_ref=part,
            send_sem=plane_send.at[jnp.where(target_chip > chip, 1, 0), source_chip, gl],
            recv_sem=plane_recv.at[source_chip, gl],
            device_id=(target_chip * 2 + core, si),
            device_id_type=MESH,
        )

    def swap_copy(source_chip, gl):
        part = tbuf.at[source_chip * 2 + core, gl]
        return pltpu.make_async_remote_copy(
            src_ref=part,
            dst_ref=part,
            send_sem=swap_send.at[source_chip, gl],
            recv_sem=plane_recv.at[source_chip, gl],
            device_id=(ti, beside),
            device_id_type=MESH,
        )

    def part_copy(source_chip, gl, side):
        part = tbuf.at[source_chip * 2 + side, gl]
        return pltpu.make_async_remote_copy(
            src_ref=part,
            dst_ref=part,
            send_sem=part_send.at[source_chip, gl],
            recv_sem=part_recv.at[source_chip, gl],
            device_id=(chip * 2 + 1 - core, si),
            device_id_type=MESH,
        )

    def dual_copy(s):
        return pltpu.make_async_remote_copy(
            src_ref=dbuf.at[si],
            dst_ref=dbuf.at[si],
            send_sem=dual_send.at[s],
            recv_sem=dual_recv.at[si],
            device_id=(ti, s),
            device_id_type=MESH,
        )

    def dual_arrival(s):
        return pltpu.make_async_remote_copy(
            src_ref=dbuf.at[s],
            dst_ref=dbuf.at[s],
            send_sem=dual_send.at[s],
            recv_sem=dual_recv.at[s],
            device_id=(ti, s),
            device_id_type=MESH,
        )

    def label_copy(t):
        return pltpu.make_async_remote_copy(
            src_ref=lbuf.at[ti],
            dst_ref=lbuf.at[ti],
            send_sem=label_send,
            recv_sem=label_recv,
            device_id=(t, si),
            device_id_type=MESH,
        )

    def label_all():
        slots = lbuf.at[pl.ds(0, nt - 1)]
        return pltpu.make_async_remote_copy(
            src_ref=slots,
            dst_ref=slots,
            send_sem=label_send,
            recv_sem=label_recv,
            device_id=(chip * 2 + 1 - core, si),
            device_id_type=MESH,
        )

    def k_copy(t, s):
        return pltpu.make_async_remote_copy(
            src_ref=kbuf.at[me],
            dst_ref=kbuf.at[me],
            send_sem=k_send,
            recv_sem=k_recv,
            device_id=(t, s),
            device_id_type=MESH,
        )

    def k_all():
        others_slots = kbuf.at[pl.ds(0, ndev - 1)]
        return pltpu.make_async_remote_copy(
            src_ref=others_slots,
            dst_ref=others_slots,
            send_sem=k_send,
            recv_sem=k_recv,
            device_id=(1 - core + chip * 2, si),
            device_id_type=MESH,
        )

    pool = pool_hbm.shape[1] * SUB
    loads[0].wait()
    picks = [lax.rem(index_ref[t], pool) for t in range(own_t)]
    for channel in range(CHANNELS):
        loads[4 + channel].wait()
        for gl in range(groups_own):
            natural = [
                pool_refs[channel][at // SUB, :, pl.ds(at % SUB, 1), :].reshape(SUB, LANES)
                for at in picks[gl * PACK : (gl + 1) * PACK]
            ]
            phases = interleave(natural, mask)
            for k in range(PACK):
                tbuf[ti, gl, channel * PACK + k] = phases[k]

    below = jnp.where(chip > 0, 1, 0)
    above = jnp.where(chip < chips - 1, 1, 0)
    pl.semaphore_wait(barrier, ns + below + above)

    def spread_out(source, gl, up, down):
        pl.when(up)(lambda: plane_copy(source, gl, chip + 1).start())
        pl.when(down)(lambda: plane_copy(source, gl, chip - 1).start())

    for gl in carried:
        spread_out(chip, gl, chip < chips - 1, chip > 0)
    for gl in range(groups_own):
        part_copy(chip, gl, core).start()

    loads[2].wait()

    def send_dual(step, carry):
        dual_copy(lax.rem(si + step, ns)).start()
        return carry

    lax.fori_loop(1, ns, send_dual, 0)

    loads[3].wait()
    for m in range(own_s):
        reps = []
        for channel in range(CHANNELS):
            phases = replicate(support_ref[channel, :, m, :], mask)
            reps.append(phases)
            for k in range(PACK):
                srep[channel, k, m] = phases[k]
        levels = levels_of(reps, mask)
        for layer in range(LAYERS):
            for k in range(PACK):
                inverse = lax.rsqrt(levels[layer][k])
                sroot[layer, 0, k, m] = inverse * (1.0 / 9.0**layer)
                sroot[layer, 1, k, m] = levels[layer][k] * inverse * (9.0**layer / math.pi)
                shalf[layer, k, m] = inverse * (1.0 / math.pi)

    def layer_map(g, layer, cross, inverse, root):
        mapped = []
        for k in range(PACK):
            x = cross[k] * (inverse[k][None] * sroot[layer, 0, k])
            size = jnp.abs(x) if layer == 0 else x
            gap = jnp.maximum(1.0 - size, 1e-20)
            rest = 1.0 + size
            half = gap * lax.rsqrt(gap)
            poly = size * (ACOS[-1] / math.pi) + ACOS[-2] / math.pi
            for term in ACOS[-3::-1]:
                poly = poly * size + term / math.pi
            near = half * poly
            slope = jnp.where(x >= 0.0, 1.0 - near, near) if layer == 0 else 1.0 - near
            sine = half * (rest * lax.rsqrt(rest))
            scaled = sine * root[k][None]
            amp[g, layer, k] = scaled
            ang[g, layer, k] = slope
            mapped.append(scaled * sroot[layer, 1, k] + slope * cross[k])
        return mapped

    def next_cross(mapped, layer):
        return [v + BETA * 9.0**layer for v in box_sum(mapped, mask)]

    def finish_group(g, at):
        cross = [mid[k] for k in range(PACK)]
        for layer in range(1, LAYERS):
            inverse = [tlev[at, layer - 1, 0, k] for k in range(PACK)]
            root = [tlev[at, layer - 1, 1, k] for k in range(PACK)]
            mapped = layer_map(g, layer, cross, inverse, root)
            if layer + 1 < LAYERS:
                cross = next_cross(mapped, layer + 1)
        total = (mapped[0] + mapped[1]) + (mapped[2] + mapped[3])
        ksum[:, pl.ds(g, 1), :] = jnp.sum(total, axis=1, keepdims=True)

    def begin_group(owner, gl, at):
        g = owner * groups_own + gl
        image = [
            [tbuf[owner, gl, channel * PACK + k] for k in range(PACK)]
            for channel in range(CHANNELS)
        ]
        levels = levels_of(image, mask)
        inverse = [[lax.rsqrt(levels[layer][k]) for k in range(PACK)] for layer in range(LAYERS)]
        root = [
            [levels[layer][k] * inverse[layer][k] for k in range(PACK)] for layer in range(LAYERS)
        ]
        for layer in range(1, LAYERS):
            for k in range(PACK):
                tlev[at, layer - 1, 0, k] = inverse[layer][k]
                tlev[at, layer - 1, 1, k] = root[layer][k]
        current = []
        for k in range(PACK):
            total = image[0][k][None] * srep[0, k]
            for channel in range(1, CHANNELS):
                total = total + image[channel][k][None] * srep[channel, k]
            current.append(total)
        cross = [v * (1.0 / 27.0) + BETA for v in box_sum(current, mask)]
        cross = next_cross(layer_map(g, 0, cross, inverse[0], root[0]), 1)
        for k in range(PACK):
            mid[k] = cross[k]

    def order(n):
        both = jnp.minimum(chip, chips - 1 - chip)
        h = (n + 1) // 2
        two_sided = jnp.where(n % 2 == 1, chip - h, chip + h)
        far = n - both
        one_sided = jnp.where(chip <= chips - 1 - chip, chip + far, chip - far)
        return jnp.where(n <= 2 * both, two_sided, one_sided)

    def place(slot):
        own = 2 * groups_own
        if share == 1:
            kind = lax.rem(slot, own)
            return slot // own, kind // groups_own, lax.rem(kind, groups_own), kind < groups_own
        reps = groups_own // 2
        r = lax.rem(slot, reps)
        step = slot // reps
        after = step - 6
        first = step < 4
        second = (step >= 4) & (step < 6)
        last = step >= 4 * chips - 2
        kind = lax.rem(after, 4)
        late = jnp.where(first, step % 2, jnp.where(second, 0, jnp.where(last, 1, kind % 2)))
        far = jnp.where(first, step // 2, jnp.where(second | last, step % 2, kind // 2))
        n = jnp.where(first, 0, jnp.where(second, 1, jnp.where(last, chips - 1, 2 + after // 4 - kind % 2)))
        return n, far, r * 2 + lax.rem(si + late, 2), late == 0

    def visit(slot, carry):
        before, at_before = carry
        n, far, gl, direct = place(slot)
        p = order(n)

        @pl.when((n > 0) & (far == 0))
        def _():
            plane_copy(p, gl, chip).wait_recv()

            @pl.when(direct)
            def _():
                spread_out(p, gl, (p < chip) & (chip < chips - 1), (p > chip) & (chip > 0))
                if share == 2:
                    swap_copy(p, gl).start()

            part_copy(p, gl, core).start()

        @pl.when(far == 1)
        def _():
            part_copy(p, gl, 1 - core).wait_recv()

        owner = p * 2 + jnp.where(far == 0, core, 1 - core)
        at = lax.rem(slot, 2)
        finish_group(before, at_before)
        begin_group(owner, gl, at)
        return owner * groups_own + gl, at

    for k in range(PACK):
        mid[k] = jnp.ones((own_s, SUB, LANES), jnp.float32)
        for layer in range(1, LAYERS):
            for which in range(2):
                tlev[1, layer - 1, which, k] = jnp.ones((SUB, LANES), jnp.float32)
    finish_group(*lax.fori_loop(0, groups, visit, (ti * groups_own, 1)))

    loads[1].wait()
    row = lax.broadcasted_iota(jnp.int32, (SUB, LANES), 0)
    lane = lax.broadcasted_iota(jnp.int32, (SUB, LANES), 1)
    line = lax.broadcasted_iota(jnp.int32, (1, LANES), 1)
    label = jnp.zeros((SUB, LANES), jnp.int32)
    labels = jnp.zeros((1, LANES), jnp.int32)
    for r in range(own_t):
        value = label_ref[r]
        label = jnp.where(row == r, value, label)
        labels = jnp.where(line == ti * own_t + r, value, labels)
    own_onehot = jnp.where(label == lane, 1.0, 0.0).astype(jnp.float32)
    lbuf[ti] = labels

    def send_label(step, carry):
        label_copy(lax.rem(ti + step, nt)).start()
        return carry

    lax.fori_loop(1, nt, send_label, 0)

    nt_dims = (((1,), (1,)), ((), ()))
    keep_g = lax.broadcasted_iota(jnp.int32, (groups, targets), 0)
    keep_t = lax.broadcasted_iota(jnp.int32, (groups, targets), 1)
    keep = jnp.where(keep_t // PACK == keep_g, 1.0, 0.0).astype(jnp.float32)
    wide_row = lax.broadcasted_iota(jnp.int32, (3 * LANES, targets), 0)
    wide_col = lax.broadcasted_iota(jnp.int32, (3 * LANES, targets), 1)
    gathers = jnp.where(wide_col % PACK == (wide_row % LANES) // SIDE, 1.0, 0.0).astype(jnp.bfloat16)
    lane_sums = jnp.dot(
        split_rows(ksum[...].reshape(own_s * groups, LANES)), gathers,
        preferred_element_type=jnp.float32,
    ) * (1.0 / (PIXELS * 9.0 ** (LAYERS - 1)))
    picked = jnp.sum(lane_sums.reshape(own_s, groups, targets) * keep[None], axis=1)
    kbuf[me] = picked

    others(lambda t, s: k_copy(t, s).start())

    part_s = 2 if own_s % 2 == 0 else own_s
    parts = own_s // part_s
    items = groups * parts

    def pair_stage(item, stage):
        item = jnp.clip(item, 0, items - 1)
        g = item // parts
        some = pl.ds((item % parts) * part_s, part_s)
        layer = LAYERS - 1 - stage
        term = [amp[g, layer, k, some] * shalf[layer, k, some] for k in range(PACK)]
        slope = [ang[g, layer, k, some] for k in range(PACK)]
        if stage > 0:
            term = [t * held[stage - 1, 0, k] + held[stage - 1, 1, k] for k, t in enumerate(term)]
            slope = [v * held[stage - 1, 0, k] for k, v in enumerate(slope)]
        level = box_sum(term, mask)
        passed = box_sum(slope, mask)
        if stage + 1 < LAYERS:
            for k in range(PACK):
                held[stage, 0, k] = passed[k]
                held[stage, 1, k] = level[k]
            return
        owner = g // groups_own
        gl = g % groups_own
        for channel in range(CHANNELS):
            for k in range(PACK):
                image = tbuf[owner, gl, channel * PACK + k]
                unit[g, channel, k, some] = (
                    passed[k] * image[None] + srep[channel, k, some] * level[k]
                )

    for stage in range(LAYERS - 1):
        for which in range(2):
            for k in range(PACK):
                held[stage, which, k] = jnp.zeros((part_s, SUB, LANES), jnp.float32)

    def pair_unit(step, carry):
        for stage in range(LAYERS - 1, -1, -1):
            pair_stage(step - stage, stage)
        return carry

    lax.fori_loop(0, items + LAYERS - 1, pair_unit, 0)

    def take_dual(step, carry):
        dual_arrival(lax.rem(si + step, ns)).wait_recv()
        return carry

    lax.fori_loop(1, ns, take_dual, 0)
    duals = dbuf[...].reshape(ns * dual_hbm.shape[0], CLASSES)
    own_duals = dbuf[si, pl.ds(ti * own_s, own_s), :]
    gram = lax.dot_general(
        own_duals, duals, nt_dims, precision=HIGH, preferred_element_type=jnp.float32
    )
    label_all().wait_recv()
    named = lbuf[0]
    for t in range(1, nt):
        named = named + lbuf[t]
    classes = lax.broadcasted_iota(jnp.int32, (CLASSES, targets), 0)
    onehot = jnp.where(classes == named[:, :targets], 1.0, 0.0).astype(jnp.float32)
    offset = jnp.dot(own_duals, onehot, precision=HIGH, preferred_element_type=jnp.float32)

    for gl in carried:
        for target, there in ((chip + 1, chip < chips - 1), (chip - 1, chip > 0)):
            pl.when(there)(functools.partial(lambda gl, target: plane_copy(chip, gl, target).wait_send(), gl, target))
    for gl in range(groups_own):
        part_copy(chip, gl, core).wait_send()

    def drain(n, carry):
        p = order(n)
        for gl in carried:
            pl.when((p < chip) & (chip < chips - 1))(
                functools.partial(lambda gl: plane_copy(p, gl, chip + 1).wait_send(), gl)
            )
            pl.when((p > chip) & (chip > 0))(
                functools.partial(lambda gl: plane_copy(p, gl, chip - 1).wait_send(), gl)
            )
            if share == 2:
                swap_copy(p, gl).wait_send()
        for gl in range(groups_own):
            part_copy(p, gl, core).wait_send()
        return carry

    lax.fori_loop(1, chips, drain, 0)

    def drain_dual(step, carry):
        dual_copy(lax.rem(si + step, ns)).wait_send()
        return carry

    lax.fori_loop(1, ns, drain_dual, 0)
    label_all().wait_send()
    k_all().wait_send()

    spread_row = lax.broadcasted_iota(jnp.int32, (3 * targets, LANES), 0)
    spread_lane = lax.broadcasted_iota(jnp.int32, (3 * targets, LANES), 1)
    spread = jnp.where(spread_row % PACK == spread_lane // SIDE, 1.0, 0.0).astype(jnp.bfloat16)

    k_all().wait_recv()
    columns = jnp.concatenate([kbuf[d] for d in range(ndev)], axis=0)
    weight = jnp.dot(gram, columns, precision=HIGH, preferred_element_type=jnp.float32) - offset
    weight = weight * (1.0 / (CHANNELS * 9.0**LAYERS))
    wide = (weight[:, None, :] * keep[None]).reshape(own_s * groups, targets)
    wexp[...] = jnp.dot(split_rows(wide), spread, preferred_element_type=jnp.float32)
    pred[...] = columns.T

    def gather_grad(first):
        pairs = [(channel, k) for channel in range(CHANNELS) for k in (first, first + 1)]

        def body(g, sums):
            w = [wexp[pl.ds(m * groups + g, SUB, stride=0), :] for m in range(own_s)]
            return tuple(
                tuple(total[m] + w[m] * unit[g, channel, k, m] for m in range(own_s))
                for total, (channel, k) in zip(sums, pairs)
            )

        zero = jnp.zeros((SUB, LANES), jnp.float32)
        sums = lax.fori_loop(0, groups, body, ((zero,) * own_s,) * len(pairs))
        return {pair: jnp.stack(total) for pair, total in zip(pairs, sums)}

    even = mask[4] % 2 == 0
    early = mask[4] < 2
    low = gather_grad(0)
    low = [fold(low[channel, 0], low[channel, 1], even, SIDE) for channel in range(CHANNELS)]
    high = gather_grad(2)
    high = [fold(high[channel, 2], high[channel, 3], even, SIDE) for channel in range(CHANNELS)]
    residual_ref[...] = jnp.dot(
        pred[pl.ds(ti * own_t, own_t), :], duals, precision=HIGH, preferred_element_type=jnp.float32
    ) - own_onehot[:own_t, :CLASSES]
    for channel in range(CHANNELS):
        flat[channel] = fold(low[channel], high[channel], early, 2 * SIDE)
        for s in range(SUB):
            grad_ref[channel, s] = flat[channel, :, s, :]


def hand_over(residual_ref, grad_ref, residual_out, grad_out):
    residual_out[...] = residual_ref[...]
    grad_out[...] = grad_ref[...]


def shards(nt, ns, target_pool, target_index, target_labels, dual_weights, support_images):
    own_t = target_index.shape[0]
    own_s = support_images.shape[0]
    groups_own = own_t // PACK
    groups = nt * groups_own
    chips = nt // 2
    ndev = nt * ns
    f32 = jnp.float32
    vmem = pl.BlockSpec(memory_space=pltpu.VMEM)
    hbm = pl.BlockSpec(memory_space=pltpu.HBM)
    dma = pltpu.SemaphoreType.DMA
    tile = (SUB, LANES)
    pool = target_pool.reshape(-1, SUB, CHANNELS, SUB, LANES).transpose(2, 0, 3, 1, 4)
    support = support_images.reshape(own_s, CHANNELS, SUB, LANES).transpose(1, 2, 0, 3)
    residual, grad = pl.pallas_call(
        functools.partial(kernel, nt, ns, own_t, own_s),
        out_shape=(
            jax.ShapeDtypeStruct((own_t, CLASSES), f32),
            jax.ShapeDtypeStruct((CHANNELS, SUB, own_s, LANES), f32),
        ),
        in_specs=[hbm] * 5,
        out_specs=(vmem, vmem),
        scratch_shapes=[
            pltpu.SMEM((own_t,), jnp.int32),
            pltpu.SMEM((own_t,), jnp.int32),
            *[pltpu.VMEM(pool.shape[1:], f32)] * CHANNELS,
            pltpu.VMEM(support.shape, f32),
            pltpu.VMEM((nt, groups_own, CHANNELS * PACK) + tile, f32),
            pltpu.VMEM((ns,) + dual_weights.shape, f32),
            pltpu.VMEM((nt, 1, LANES), jnp.int32),
            pltpu.VMEM((ndev, own_s, nt * own_t), f32),
            pltpu.VMEM((CHANNELS, PACK, own_s) + tile, f32),
            pltpu.VMEM((LAYERS, 2, PACK, own_s) + tile, f32),
            pltpu.VMEM((LAYERS, PACK, own_s) + tile, f32),
            pltpu.VMEM((2, LAYERS - 1, 2, PACK) + tile, f32),
            pltpu.VMEM((PACK, own_s) + tile, f32),
            pltpu.VMEM((LAYERS - 1, 2, PACK, 2 if own_s % 2 == 0 else own_s) + tile, f32),
            pltpu.VMEM((groups, LAYERS, PACK, own_s) + tile, f32),
            pltpu.VMEM((groups, LAYERS, PACK, own_s) + tile, f32),
            pltpu.VMEM((groups, CHANNELS, PACK, own_s) + tile, f32),
            pltpu.VMEM((own_s, groups, LANES), f32),
            pltpu.VMEM((own_s * groups, LANES), f32),
            pltpu.VMEM((nt * own_t, ns * dual_weights.shape[0]), f32),
            pltpu.VMEM((CHANNELS, own_s) + tile, f32),
            dma((4 + CHANNELS,)),
            dma((2, chips, groups_own)),
            dma((chips, groups_own)),
            dma((chips, groups_own)),
            dma((chips, groups_own)),
            dma((chips, groups_own)),
            dma((ns,)),
            dma((ns,)),
            dma,
            dma,
            dma,
            dma,
        ],
        compiler_params=pltpu.CompilerParams(
            collective_id=0, has_side_effects=True, vmem_limit_bytes=44 * 2**20
        ),
    )(*[
        pltpu.with_memory_space_constraint(v, pltpu.HBM)
        for v in (target_index, target_labels, pool, dual_weights, support)
    ])
    residual, grad = pl.pallas_call(
        hand_over,
        out_shape=(
            jax.ShapeDtypeStruct(residual.shape, f32),
            jax.ShapeDtypeStruct(grad.shape, f32),
        ),
        in_specs=[vmem, vmem],
        out_specs=(vmem, vmem),
        compiler_params=pltpu.CompilerParams(vmem_limit_bytes=2**20),
    )(residual, grad)
    return (residual, grad.transpose(2, 0, 1, 3).reshape(support_images.shape))


def solution(mesh):
    in_specs = (
        P("tgt", None, None),
        P("tgt"),
        P("tgt"),
        P("sup", None),
        P(("sup", "tgt"), None, None),
    )
    out_specs = (P("tgt", None), P(("sup", "tgt"), None, None))
    body = functools.partial(shards, mesh.shape["tgt"], mesh.shape["sup"])
    return jax.shard_map(body, mesh=mesh, in_specs=in_specs, out_specs=out_specs, check_vma=False)
```

```python
import functools
import math

import jax
import jax.numpy as jnp
from jax import lax
from jax.experimental import pallas as pl
from jax.experimental.pallas import tpu as pltpu
from jax.sharding import PartitionSpec as P

CHANNELS = 3
SIDE = 32
CLASSES = 100
LAYERS = 3
PIXELS = 1024
BETA = 0.01
PACK = 4
SUB = 8
LANES = 128
MESH = pl.DeviceIdType.MESH
HIGH = lax.Precision.HIGHEST
ACOS = (
    1.5707956895,
    -0.2145428158,
    0.0881710453,
    -0.0459272047,
    0.0206200335,
    -0.0049111629,
)


STRETCH = (-ACOS[-1] / math.pi) ** (2.0 / (2 * len(ACOS) - 1))
MONIC = [
    term / ACOS[-1] * STRETCH ** (len(ACOS) - 1 - power) for power, term in enumerate(ACOS)
][:-1]


def masks():
    lane = lax.broadcasted_iota(jnp.int32, (SUB, LANES), 1)
    row = lax.broadcasted_iota(jnp.int32, (SUB, LANES), 0)
    column = lane % SIDE
    return (column > 0, column < SIDE - 1, row > 0, row < SUB - 1, lane // SIDE)


def box_sum(maps, mask):
    right, left, down, up, _ = mask
    axis = maps[0].ndim - 1

    def across(v):
        return (
            v
            + jnp.where(right, pltpu.roll(v, 1, axis), 0.0)
            + jnp.where(left, pltpu.roll(v, LANES - 1, axis), 0.0)
        )

    before = jnp.where(down, pltpu.roll(maps[3], 1, axis - 1), 0.0)
    after = jnp.where(up, pltpu.roll(maps[0], SUB - 1, axis - 1), 0.0)
    low = maps[0] + maps[1]
    high = maps[2] + maps[3]
    return [across(v) for v in (before + low, low + maps[2], maps[1] + high, high + after)]


def vertical(maps, mask):
    down, up = mask[2], mask[3]
    axis = maps[0].ndim - 2
    before = jnp.where(down, pltpu.roll(maps[3], 1, axis), 0.0)
    after = jnp.where(up, pltpu.roll(maps[0], SUB - 1, axis), 0.0)
    low = maps[0] + maps[1]
    high = maps[2] + maps[3]
    return [before + low, low + maps[2], maps[1] + high, high + after]


def band_sum(maps, mask, band):
    return across(vertical(maps, mask), band)


def across(maps, band):
    shape = maps[0].shape
    rows = jnp.stack(maps).reshape(-1, LANES)
    high = rows.astype(jnp.bfloat16)
    low = (rows - high.astype(jnp.float32)).astype(jnp.bfloat16)
    out = jnp.dot(
        jnp.concatenate([high, low], axis=1), band[...], preferred_element_type=jnp.float32
    ).reshape((len(maps),) + shape)
    return [out[k] for k in range(len(maps))]


def interleave(images, mask):
    group = mask[4]
    out = []
    for k in range(PACK):
        total = None
        for m in range(PACK):
            shift = ((m - k) * SIDE) % LANES
            moved = images[m] if shift == 0 else pltpu.roll(images[m], shift, 1)
            total = moved if total is None else jnp.where(group == m, moved, total)
        out.append(total)
    return out


def replicate(image, mask):
    group = mask[4]
    out = []
    rolled = [image] + [pltpu.roll(image, SIDE * s, 1) for s in range(1, PACK)]
    for k in range(PACK):
        total = None
        for m in range(PACK):
            moved = rolled[(m - k) % PACK]
            total = moved if total is None else jnp.where(group == m, moved, total)
        out.append(total)
    return out


def levels_of(images, mask):
    energy = []
    for k in range(PACK):
        total = images[0][k] * images[0][k]
        for channel in range(1, CHANNELS):
            total = total + images[channel][k] * images[channel][k]
        energy.append(total * (1.0 / CHANNELS))
    levels = []
    current = energy
    for _ in range(LAYERS):
        current = [v * (1.0 / 9.0) + BETA for v in box_sum(current, mask)]
        levels.append(current)
    return levels


def split_rows(v):
    high = v.astype(jnp.bfloat16)
    rest = v - high.astype(jnp.float32)
    middle = rest.astype(jnp.bfloat16)
    low = (rest - middle.astype(jnp.float32)).astype(jnp.bfloat16)
    return jnp.concatenate([high, middle, low], axis=1)


def fold(a, b, keep, shift):
    return jnp.where(keep, a, b) + pltpu.roll(jnp.where(keep, b, a), shift, a.ndim - 1)


def kernel(
    nt, ns, own_t, own_s,
    index_hbm, label_hbm, pool_hbm, dual_hbm, support_hbm,
    residual_ref, grad_ref,
    index_ref, label_ref, pool_a, pool_b, pool_c, support_ref,
    tbuf, dbuf, lbuf, kbuf, band, gathers, spread, keep, srep, sroot, shalf, tlev, mid, held, amp, ang, unit, ksum, wexp, pred, flat,
    in_sem, plane_send, plane_recv, swap_send, part_send, part_recv,
    dual_send, dual_recv, label_send, label_recv, k_send, k_recv,
):
    ti = lax.axis_index("tgt")
    si = lax.axis_index("sup")
    pool_refs = (pool_a, pool_b, pool_c)
    chips = nt // 2
    chip = ti // 2
    core = ti % 2
    ndev = nt * ns
    me = si * nt + ti
    groups_own = own_t // PACK
    groups = nt * groups_own
    targets = nt * own_t
    mask = masks()
    share = 2 if groups_own % 2 == 0 and ns % 2 == 0 else 1
    beside = si + 1 - 2 * (si % 2)
    barrier = pltpu.get_barrier_semaphore()

    def others(action):
        for s in range(ns):
            for t in range(nt):
                pl.when((si != s) | (ti != t))(functools.partial(action, t, s))

    def greet(t, s):
        pl.semaphore_signal(barrier, inc=1, device_id=(t, s), device_id_type=MESH)

    for step in range(1, ns):
        greet(ti, lax.rem(si + step, ns))
    greet(chip * 2 + 1 - core, si)
    for step in range(1, chips):
        greet(lax.rem(ti + 2 * step, nt), si)

    def fetch(at, src, dst):
        return pltpu.make_async_copy(src, dst, in_sem.at[at])

    loads = [
        fetch(0, index_hbm, index_ref),
        fetch(1, label_hbm, label_ref),
        fetch(2, dual_hbm, dbuf.at[si]),
        fetch(3, support_hbm, support_ref),
    ] + [fetch(4 + c, pool_hbm.at[c], pool_refs[c]) for c in range(CHANNELS)]
    for at in (3, 0, 4, 5, 6, 2, 1):
        loads[at].start()

    def plane_copy(source_chip, gl, target_chip):
        part = tbuf.at[source_chip * 2 + core, gl]
        return pltpu.make_async_remote_copy(
            src_ref=part,
            dst_ref=part,
            send_sem=plane_send.at[target_chip, gl],
            recv_sem=plane_recv.at[source_chip, gl],
            device_id=(target_chip * 2 + core, si),
            device_id_type=MESH,
        )

    def swap_copy(source_chip, gl):
        part = tbuf.at[source_chip * 2 + core, gl]
        return pltpu.make_async_remote_copy(
            src_ref=part,
            dst_ref=part,
            send_sem=swap_send.at[source_chip, gl],
            recv_sem=plane_recv.at[source_chip, gl],
            device_id=(ti, beside),
            device_id_type=MESH,
        )

    def part_copy(source_chip, gl, side):
        part = tbuf.at[source_chip * 2 + side, gl]
        return pltpu.make_async_remote_copy(
            src_ref=part,
            dst_ref=part,
            send_sem=part_send.at[source_chip, gl],
            recv_sem=part_recv.at[source_chip, gl],
            device_id=(chip * 2 + 1 - core, si),
            device_id_type=MESH,
        )

    def dual_copy(s):
        return pltpu.make_async_remote_copy(
            src_ref=dbuf.at[si],
            dst_ref=dbuf.at[si],
            send_sem=dual_send.at[s],
            recv_sem=dual_recv.at[si],
            device_id=(ti, s),
            device_id_type=MESH,
        )

    def dual_arrival(s):
        return pltpu.make_async_remote_copy(
            src_ref=dbuf.at[s],
            dst_ref=dbuf.at[s],
            send_sem=dual_send.at[s],
            recv_sem=dual_recv.at[s],
            device_id=(ti, s),
            device_id_type=MESH,
        )

    def label_copy(t):
        return pltpu.make_async_remote_copy(
            src_ref=lbuf.at[ti],
            dst_ref=lbuf.at[ti],
            send_sem=label_send,
            recv_sem=label_recv,
            device_id=(t, si),
            device_id_type=MESH,
        )

    def label_all():
        slots = lbuf.at[pl.ds(0, nt - 1)]
        return pltpu.make_async_remote_copy(
            src_ref=slots,
            dst_ref=slots,
            send_sem=label_send,
            recv_sem=label_recv,
            device_id=(chip * 2 + 1 - core, si),
            device_id_type=MESH,
        )

    def k_copy(t, s):
        return pltpu.make_async_remote_copy(
            src_ref=kbuf.at[me],
            dst_ref=kbuf.at[me],
            send_sem=k_send,
            recv_sem=k_recv,
            device_id=(t, s),
            device_id_type=MESH,
        )

    def k_all():
        others_slots = kbuf.at[pl.ds(0, ndev - 1)]
        return pltpu.make_async_remote_copy(
            src_ref=others_slots,
            dst_ref=others_slots,
            send_sem=k_send,
            recv_sem=k_recv,
            device_id=(1 - core + chip * 2, si),
            device_id_type=MESH,
        )

    band_row = lax.broadcasted_iota(jnp.int32, (LANES, LANES), 0)
    band_col = lax.broadcasted_iota(jnp.int32, (LANES, LANES), 1)
    near = (jnp.abs(band_row - band_col) <= 1) & (band_row // SIDE == band_col // SIDE)
    near = jnp.where(near, 1.0, 0.0).astype(jnp.bfloat16)
    for part in range(2):
        band[pl.ds(part * LANES, LANES), :] = near
    wide_row = lax.broadcasted_iota(jnp.int32, (LANES, targets), 0)
    wide_col = lax.broadcasted_iota(jnp.int32, (LANES, targets), 1)
    into = jnp.where(wide_col % PACK == wide_row // SIDE, 1.0, 0.0).astype(jnp.bfloat16)
    tall_row = lax.broadcasted_iota(jnp.int32, (targets, LANES), 0)
    tall_col = lax.broadcasted_iota(jnp.int32, (targets, LANES), 1)
    onto = jnp.where(tall_row % PACK == tall_col // SIDE, 1.0, 0.0).astype(jnp.bfloat16)
    for part in range(3):
        gathers[pl.ds(part * LANES, LANES), :] = into
        spread[pl.ds(part * targets, targets), :] = onto
    keep_g = lax.broadcasted_iota(jnp.int32, (groups, targets), 0)
    keep_t = lax.broadcasted_iota(jnp.int32, (groups, targets), 1)
    keep[...] = jnp.where(keep_t // PACK == keep_g, 1.0, 0.0).astype(jnp.float32)
    loads[3].wait()
    for m in range(own_s):
        reps = []
        for channel in range(CHANNELS):
            phases = replicate(support_ref[channel, :, m, :], mask)
            reps.append(phases)
            for k in range(PACK):
                srep[channel, k, m] = phases[k] * (1.0 / (9.0 * CHANNELS))
        levels = levels_of(reps, mask)
        for layer in range(LAYERS):
            for k in range(PACK):
                inverse = lax.rsqrt(levels[layer][k])
                sroot[layer, 0, k, m] = inverse * (STRETCH / 9.0**layer)
                sroot[layer, 1, k, m] = levels[layer][k] * inverse * (9.0**layer / (STRETCH * math.pi))
                shalf[layer, k, m] = inverse * (9.0 * CHANNELS / (STRETCH * math.pi))

    pool = pool_hbm.shape[1] * SUB
    loads[0].wait()
    picks = [lax.rem(index_ref[t], pool) for t in range(own_t)]
    for channel in range(CHANNELS):
        loads[4 + channel].wait()
        for gl in range(groups_own):
            natural = [
                pool_refs[channel][at // SUB, :, pl.ds(at % SUB, 1), :].reshape(SUB, LANES)
                for at in picks[gl * PACK : (gl + 1) * PACK]
            ]
            phases = interleave(natural, mask)
            for k in range(PACK):
                tbuf[ti, gl, channel * PACK + k] = phases[k]

    pl.semaphore_wait(barrier, ns + chips - 1)

    def choice(h):
        return lax.rem(si + h, groups_own)

    def each_plane(action):
        for h in range(0, groups_own, share):
            for step in range(chips - 1, 0, -1):
                for target in (chip + step, chip - step):
                    pl.when((target >= 0) & (target < chips))(
                        functools.partial(action, choice(h), target)
                    )

    each_plane(lambda gl, target: plane_copy(chip, gl, target).start())
    for gl in range(groups_own):
        part_copy(chip, gl, core).start()

    loads[2].wait()

    def send_dual(step, carry):
        dual_copy(lax.rem(si + step, ns)).start()
        return carry

    lax.fori_loop(1, ns, send_dual, 0)

    def layer_map(g, layer, cross, inverse, root):
        mapped = []
        for k in range(PACK):
            x = cross[k] * (inverse[k][None] * sroot[layer, 0, k])
            size = jnp.abs(x) if layer == 0 else x
            gap = jnp.maximum(STRETCH - size, 1e-20)
            rest = STRETCH + size
            half = gap * lax.rsqrt(gap)
            poly = size + MONIC[-1]
            for term in MONIC[-2::-1]:
                poly = poly * size + term
            bend = half * poly
            slope = jnp.where(x >= 0.0, 1.0 + bend, 0.0 - bend) if layer == 0 else 1.0 + bend
            sine = half * (rest * lax.rsqrt(rest))
            scaled = sine * root[k][None]
            amp[g, layer, k] = scaled
            ang[g, layer, k] = slope
            mapped.append(scaled * sroot[layer, 1, k] + slope * cross[k])
        return mapped

    def next_cross(mapped, layer):
        return [v + BETA * 9.0**layer for v in band_sum(mapped, mask, band)]

    def finish_group(g, at, j):
        cross = [v + BETA * 9.0 for v in across([mid[j, k] for k in range(PACK)], band)]
        for layer in range(1, LAYERS):
            inverse = [tlev[at, j, layer - 1, 0, k] for k in range(PACK)]
            root = [tlev[at, j, layer - 1, 1, k] for k in range(PACK)]
            mapped = layer_map(g, layer, cross, inverse, root)
            if layer + 1 < LAYERS:
                cross = next_cross(mapped, layer + 1)
        total = (mapped[0] + mapped[1]) + (mapped[2] + mapped[3])
        ksum[:, pl.ds(g, 1), :] = jnp.sum(total, axis=1, keepdims=True)

    def begin_group(owner, gl, at, j):
        g = owner * groups_own + gl
        image = [
            [tbuf[owner, gl, channel * PACK + k] for k in range(PACK)]
            for channel in range(CHANNELS)
        ]
        levels = levels_of(image, mask)
        inverse = [[lax.rsqrt(levels[layer][k]) for k in range(PACK)] for layer in range(LAYERS)]
        root = [
            [levels[layer][k] * inverse[layer][k] for k in range(PACK)] for layer in range(LAYERS)
        ]
        for layer in range(1, LAYERS):
            for k in range(PACK):
                tlev[at, j, layer - 1, 0, k] = inverse[layer][k]
                tlev[at, j, layer - 1, 1, k] = root[layer][k]
        current = []
        for k in range(PACK):
            total = image[0][k][None] * srep[0, k]
            for channel in range(1, CHANNELS):
                total = total + image[channel][k][None] * srep[channel, k]
            current.append(total)
        cross = [v + BETA for v in band_sum(current, mask, band)]
        summed = vertical(layer_map(g, 0, cross, inverse[0], root[0]), mask)
        for k in range(PACK):
            mid[j, k] = summed[k]

    def order(n):
        both = jnp.minimum(chip, chips - 1 - chip)
        h = (n + 1) // 2
        two_sided = jnp.where(n % 2 == 1, chip - h, chip + h)
        far = n - both
        one_sided = jnp.where(chip <= chips - 1 - chip, chip + far, chip - far)
        return jnp.where(n <= 2 * both, two_sided, one_sided)

    def block(before, old, at, fresh):
        for j, g in enumerate(before):
            finish_group(g, old, j)
        for j, (owner, gl) in enumerate(fresh):
            begin_group(owner, gl, at, j)
        return tuple(owner * groups_own + gl for owner, gl in fresh)

    def near_item(n, gl, direct):
        p = order(n)
        plane_copy(p, gl, chip).wait_recv()
        if share == 2:
            pl.when(direct)(lambda: swap_copy(p, gl).start())
        part_copy(p, gl, core).start()
        return p * 2 + core, gl

    def far_item(n, gl):
        p = order(n)
        part_copy(p, gl, 1 - core).wait_recv()
        return p * 2 + 1 - core, gl

    slots = max(chips - 1, 1)
    before = ()
    last = slots - 1
    own = [(side, h) for side in (0, 1) for h in range(groups_own)]
    for first in range(0, len(own), 2):
        fresh = [
            far_item(0, choice(h)) if side else (ti, choice(h))
            for side, h in own[first : first + 2]
        ]
        at = (first // 2 - groups_own) % slots
        before = block(before, last, at, fresh)
        last = at

    def sweep(h, before):
        gl = choice(h)
        direct = h % 2 == 0
        items = [(side, n) for side in (0, 1) for n in range(1, chips)]
        for first in range(0, len(items), 2):
            fresh = [
                far_item(n, gl) if side else near_item(n, gl, direct)
                for side, n in items[first : first + 2]
            ]
            at = first // 2
            before = block(before, (at - 1) % slots, at, fresh)
        return before

    before = lax.fori_loop(0, groups_own, sweep, before)
    block(before, slots - 1, 0, [])

    loads[1].wait()
    row = lax.broadcasted_iota(jnp.int32, (SUB, LANES), 0)
    lane = lax.broadcasted_iota(jnp.int32, (SUB, LANES), 1)
    line = lax.broadcasted_iota(jnp.int32, (1, LANES), 1)
    label = jnp.zeros((SUB, LANES), jnp.int32)
    labels = jnp.zeros((1, LANES), jnp.int32)
    for r in range(own_t):
        value = label_ref[r]
        label = jnp.where(row == r, value, label)
        labels = jnp.where(line == ti * own_t + r, value, labels)
    own_onehot = jnp.where(label == lane, 1.0, 0.0).astype(jnp.float32)
    lbuf[ti] = labels

    def send_label(step, carry):
        label_copy(lax.rem(ti + step, nt)).start()
        return carry

    lax.fori_loop(1, nt, send_label, 0)

    nt_dims = (((1,), (1,)), ((), ()))
    lane_sums = jnp.dot(
        split_rows(ksum[...].reshape(own_s * groups, LANES)), gathers[...],
        preferred_element_type=jnp.float32,
    ) * (1.0 / (PIXELS * 9.0 ** (LAYERS - 1)))
    picked = jnp.sum(lane_sums.reshape(own_s, groups, targets) * keep[...][None], axis=1)
    kbuf[me] = picked

    others(lambda t, s: k_copy(t, s).start())

    held[...] = jnp.zeros_like(held)

    def pair_unit(step, carry):
        levels = across([held[0, at, k] for at in range(LAYERS) for k in range(PACK)], band)
        passes = across([held[1, at, k] for at in range(LAYERS) for k in range(PACK)], band)

        g = jnp.clip(step - LAYERS, 0, groups - 1)
        owner = g // groups_own
        gl = g % groups_own
        last = (LAYERS - 1) * PACK
        for channel in range(CHANNELS):
            for k in range(PACK):
                image = tbuf[owner, gl, channel * PACK + k]
                unit[g, channel, k] = (
                    passes[last + k] * image[None] + srep[channel, k] * levels[last + k]
                )
        for at in range(LAYERS - 1, -1, -1):
            g = jnp.clip(step - at, 0, groups - 1)
            layer = LAYERS - 1 - at
            term = [amp[g, layer, k] * shalf[layer, k] for k in range(PACK)]
            slope = [ang[g, layer, k] for k in range(PACK)]
            if at > 0:
                start = (at - 1) * PACK
                term = [t * passes[start + k] + levels[start + k] for k, t in enumerate(term)]
                slope = [v * passes[start + k] for k, v in enumerate(slope)]
            for k, v in enumerate(vertical(term, mask)):
                held[0, at, k] = v
            for k, v in enumerate(vertical(slope, mask)):
                held[1, at, k] = v
        return carry

    lax.fori_loop(0, groups + LAYERS, pair_unit, 0)

    def take_dual(step, carry):
        dual_arrival(lax.rem(si + step, ns)).wait_recv()
        return carry

    lax.fori_loop(1, ns, take_dual, 0)
    duals = dbuf[...].reshape(ns * dual_hbm.shape[0], CLASSES)
    own_duals = dbuf[si, pl.ds(ti * own_s, own_s), :]
    gram = lax.dot_general(
        own_duals, duals, nt_dims, precision=HIGH, preferred_element_type=jnp.float32
    )
    label_all().wait_recv()
    named = lbuf[0]
    for t in range(1, nt):
        named = named + lbuf[t]
    classes = lax.broadcasted_iota(jnp.int32, (CLASSES, targets), 0)
    onehot = jnp.where(classes == named[:, :targets], 1.0, 0.0).astype(jnp.float32)
    offset = jnp.dot(own_duals, onehot, precision=HIGH, preferred_element_type=jnp.float32)

    each_plane(lambda gl, target: plane_copy(chip, gl, target).wait_send())
    for gl in range(groups_own):
        part_copy(chip, gl, core).wait_send()

    def drain(n, carry):
        p = order(n)
        for h in range(groups_own):
            if share == 2 and h % 2 == 0:
                swap_copy(p, choice(h)).wait_send()
            part_copy(p, choice(h), core).wait_send()
        return carry

    lax.fori_loop(1, chips, drain, 0)

    def drain_dual(step, carry):
        dual_copy(lax.rem(si + step, ns)).wait_send()
        return carry

    lax.fori_loop(1, ns, drain_dual, 0)
    label_all().wait_send()
    k_all().wait_send()

    k_all().wait_recv()
    columns = jnp.concatenate([kbuf[d] for d in range(ndev)], axis=0)
    weight = jnp.dot(gram, columns, precision=HIGH, preferred_element_type=jnp.float32) - offset
    weight = weight * (1.0 / (CHANNELS * 9.0**LAYERS))
    wide = (weight[:, None, :] * keep[...][None]).reshape(own_s * groups, targets)
    wexp[...] = jnp.dot(split_rows(wide), spread[...], preferred_element_type=jnp.float32)
    pred[...] = columns.T

    even = mask[4] % 2 == 0
    early = mask[4] < 2
    for m in range(own_s):
        sums = [[None] * PACK for _ in range(CHANNELS)]
        for g in range(groups):
            w = wexp[pl.ds(m * groups + g, SUB, stride=0), :]
            for channel in range(CHANNELS):
                for k in range(PACK):
                    value = w * unit[g, channel, k, m]
                    sums[channel][k] = value if g == 0 else sums[channel][k] + value
        for channel in range(CHANNELS):
            low = fold(sums[channel][0], sums[channel][1], even, SIDE)
            high = fold(sums[channel][2], sums[channel][3], even, SIDE)
            flat[channel, m] = fold(low, high, early, 2 * SIDE)
    residual_ref[...] = jnp.dot(
        pred[pl.ds(ti * own_t, own_t), :], duals, precision=HIGH, preferred_element_type=jnp.float32
    ) - own_onehot[:own_t, :CLASSES]
    for channel in range(CHANNELS):
        for s in range(SUB):
            grad_ref[channel, s] = flat[channel, :, s, :]


def hand_over(residual_ref, grad_ref, residual_out, grad_out):
    residual_out[...] = residual_ref[...]
    grad_out[...] = grad_ref[...]


def shards(nt, ns, target_pool, target_index, target_labels, dual_weights, support_images):
    own_t = target_index.shape[0]
    own_s = support_images.shape[0]
    groups_own = own_t // PACK
    groups = nt * groups_own
    chips = nt // 2
    ndev = nt * ns
    f32 = jnp.float32
    vmem = pl.BlockSpec(memory_space=pltpu.VMEM)
    hbm = pl.BlockSpec(memory_space=pltpu.HBM)
    dma = pltpu.SemaphoreType.DMA
    tile = (SUB, LANES)
    pool = target_pool.reshape(-1, SUB, CHANNELS, SUB, LANES).transpose(2, 0, 3, 1, 4)
    support = support_images.reshape(own_s, CHANNELS, SUB, LANES).transpose(1, 2, 0, 3)
    residual, grad = pl.pallas_call(
        functools.partial(kernel, nt, ns, own_t, own_s),
        out_shape=(
            jax.ShapeDtypeStruct((own_t, CLASSES), f32),
            jax.ShapeDtypeStruct((CHANNELS, SUB, own_s, LANES), f32),
        ),
        in_specs=[hbm] * 5,
        out_specs=(vmem, vmem),
        scratch_shapes=[
            pltpu.SMEM((own_t,), jnp.int32),
            pltpu.SMEM((own_t,), jnp.int32),
            *[pltpu.VMEM(pool.shape[1:], f32)] * CHANNELS,
            pltpu.VMEM(support.shape, f32),
            pltpu.VMEM((nt, groups_own, CHANNELS * PACK) + tile, f32),
            pltpu.VMEM((ns,) + dual_weights.shape, f32),
            pltpu.VMEM((nt, 1, LANES), jnp.int32),
            pltpu.VMEM((ndev, own_s, nt * own_t), f32),
            pltpu.VMEM((2 * LANES, LANES), jnp.bfloat16),
            pltpu.VMEM((3 * LANES, nt * own_t), jnp.bfloat16),
            pltpu.VMEM((3 * nt * own_t, LANES), jnp.bfloat16),
            pltpu.VMEM((groups, nt * own_t), f32),
            pltpu.VMEM((CHANNELS, PACK, own_s) + tile, f32),
            pltpu.VMEM((LAYERS, 2, PACK, own_s) + tile, f32),
            pltpu.VMEM((LAYERS, PACK, own_s) + tile, f32),
            pltpu.VMEM((max(chips - 1, 1), 2, LAYERS - 1, 2, PACK) + tile, f32),
            pltpu.VMEM((2, PACK, own_s) + tile, f32),
            pltpu.VMEM((2, LAYERS, PACK, own_s) + tile, f32),
            pltpu.VMEM((groups, LAYERS, PACK, own_s) + tile, f32),
            pltpu.VMEM((groups, LAYERS, PACK, own_s) + tile, f32),
            pltpu.VMEM((groups, CHANNELS, PACK, own_s) + tile, f32),
            pltpu.VMEM((own_s, groups, LANES), f32),
            pltpu.VMEM((own_s * groups, LANES), f32),
            pltpu.VMEM((nt * own_t, ns * dual_weights.shape[0]), f32),
            pltpu.VMEM((CHANNELS, own_s) + tile, f32),
            dma((4 + CHANNELS,)),
            dma((chips, groups_own)),
            dma((chips, groups_own)),
            dma((chips, groups_own)),
            dma((chips, groups_own)),
            dma((chips, groups_own)),
            dma((ns,)),
            dma((ns,)),
            dma,
            dma,
            dma,
            dma,
        ],
        compiler_params=pltpu.CompilerParams(
            collective_id=0, has_side_effects=True, vmem_limit_bytes=44 * 2**20
        ),
    )(*[
        pltpu.with_memory_space_constraint(v, pltpu.HBM)
        for v in (target_index, target_labels, pool, dual_weights, support)
    ])
    residual, grad = pl.pallas_call(
        hand_over,
        out_shape=(
            jax.ShapeDtypeStruct(residual.shape, f32),
            jax.ShapeDtypeStruct(grad.shape, f32),
        ),
        in_specs=[vmem, vmem],
        out_specs=(vmem, vmem),
        compiler_params=pltpu.CompilerParams(vmem_limit_bytes=2**20),
    )(residual, grad)
    return (residual, grad.transpose(2, 0, 1, 3).reshape(support_images.shape))


def solution(mesh):
    in_specs = (
        P("tgt", None, None),
        P("tgt"),
        P("tgt"),
        P("sup", None),
        P(("sup", "tgt"), None, None),
    )
    out_specs = (P("tgt", None), P(("sup", "tgt"), None, None))
    body = functools.partial(shards, mesh.shape["tgt"], mesh.shape["sup"])
    return jax.shard_map(body, mesh=mesh, in_specs=in_specs, out_specs=out_specs, check_vma=False)
```

```python
import functools
import math

import jax
import jax.numpy as jnp
from jax import lax
from jax.experimental import pallas as pl
from jax.experimental.pallas import tpu as pltpu
from jax.sharding import PartitionSpec as P

CHANNELS = 3
SIDE = 32
CLASSES = 100
LAYERS = 3
PIXELS = 1024
BETA = 0.01
PACK = 4
SUB = 8
LANES = 128
MESH = pl.DeviceIdType.MESH
HIGH = lax.Precision.HIGHEST
ACOS = (
    1.5707956895,
    -0.2145428158,
    0.0881710453,
    -0.0459272047,
    0.0206200335,
    -0.0049111629,
)


STRETCH = (-ACOS[-1] / math.pi) ** (2.0 / (2 * len(ACOS) - 1))
MONIC = [
    term / ACOS[-1] * STRETCH ** (len(ACOS) - 1 - power) for power, term in enumerate(ACOS)
][:-1]


def masks():
    lane = lax.broadcasted_iota(jnp.int32, (SUB, LANES), 1)
    row = lax.broadcasted_iota(jnp.int32, (SUB, LANES), 0)
    column = lane % SIDE
    return (column > 0, column < SIDE - 1, row > 0, row < SUB - 1, lane // SIDE)


def box_sum(maps, mask):
    right, left, down, up, _ = mask
    axis = maps[0].ndim - 1

    def across(v):
        return (
            v
            + jnp.where(right, pltpu.roll(v, 1, axis), 0.0)
            + jnp.where(left, pltpu.roll(v, LANES - 1, axis), 0.0)
        )

    before = jnp.where(down, pltpu.roll(maps[3], 1, axis - 1), 0.0)
    after = jnp.where(up, pltpu.roll(maps[0], SUB - 1, axis - 1), 0.0)
    low = maps[0] + maps[1]
    high = maps[2] + maps[3]
    return [across(v) for v in (before + low, low + maps[2], maps[1] + high, high + after)]


def vertical(maps, mask):
    down, up = mask[2], mask[3]
    axis = maps[0].ndim - 2
    before = jnp.where(down, pltpu.roll(maps[3], 1, axis), 0.0)
    after = jnp.where(up, pltpu.roll(maps[0], SUB - 1, axis), 0.0)
    low = maps[0] + maps[1]
    high = maps[2] + maps[3]
    return [before + low, low + maps[2], maps[1] + high, high + after]


def band_sum(maps, mask, band):
    return across(vertical(maps, mask), band)


def across(maps, band):
    shape = maps[0].shape
    rows = jnp.stack(maps).reshape(-1, LANES)
    high = rows.astype(jnp.bfloat16)
    low = (rows - high.astype(jnp.float32)).astype(jnp.bfloat16)
    out = jnp.dot(
        jnp.concatenate([high, low], axis=1), band[...], preferred_element_type=jnp.float32
    ).reshape((len(maps),) + shape)
    return [out[k] for k in range(len(maps))]


def interleave(images, mask):
    group = mask[4]
    out = []
    for k in range(PACK):
        total = None
        for m in range(PACK):
            shift = ((m - k) * SIDE) % LANES
            moved = images[m] if shift == 0 else pltpu.roll(images[m], shift, 1)
            total = moved if total is None else jnp.where(group == m, moved, total)
        out.append(total)
    return out


def replicate(image, mask):
    group = mask[4]
    out = []
    rolled = [image] + [pltpu.roll(image, SIDE * s, 1) for s in range(1, PACK)]
    for k in range(PACK):
        total = None
        for m in range(PACK):
            moved = rolled[(m - k) % PACK]
            total = moved if total is None else jnp.where(group == m, moved, total)
        out.append(total)
    return out


def levels_of(images, mask):
    energy = []
    for k in range(PACK):
        total = images[0][k] * images[0][k]
        for channel in range(1, CHANNELS):
            total = total + images[channel][k] * images[channel][k]
        energy.append(total * (1.0 / CHANNELS))
    levels = []
    current = energy
    for _ in range(LAYERS):
        current = [v * (1.0 / 9.0) + BETA for v in box_sum(current, mask)]
        levels.append(current)
    return levels


def split_rows(v):
    high = v.astype(jnp.bfloat16)
    rest = v - high.astype(jnp.float32)
    middle = rest.astype(jnp.bfloat16)
    low = (rest - middle.astype(jnp.float32)).astype(jnp.bfloat16)
    return jnp.concatenate([high, middle, low], axis=1)


def fold(a, b, keep, shift):
    return jnp.where(keep, a, b) + pltpu.roll(jnp.where(keep, b, a), shift, a.ndim - 1)


def kernel(
    nt, ns, own_t, own_s,
    index_hbm, label_hbm, pool_hbm, dual_hbm, support_hbm,
    residual_ref, grad_ref,
    index_ref, label_ref, pool_a, pool_b, pool_c, support_ref,
    tbuf, dbuf, lbuf, kbuf, band, gathers, spread, keep, srep, sroot, shalf, tlev, mid, held, amp, ang, unit, ksum, wexp, pred, flat,
    in_sem, plane_send, plane_recv, swap_send, part_send, part_recv,
    dual_send, dual_recv, label_send, label_recv, k_send, k_recv,
):
    ti = lax.axis_index("tgt")
    si = lax.axis_index("sup")
    pool_refs = (pool_a, pool_b, pool_c)
    chips = nt // 2
    chip = ti // 2
    core = ti % 2
    ndev = nt * ns
    me = si * nt + ti
    groups_own = own_t // PACK
    groups = nt * groups_own
    targets = nt * own_t
    mask = masks()
    share = 2 if groups_own % 2 == 0 and ns % 2 == 0 else 1
    beside = si + 1 - 2 * (si % 2)
    barrier = pltpu.get_barrier_semaphore()

    def greet(t, s):
        pl.semaphore_signal(barrier, inc=1, device_id=(t, s), device_id_type=MESH)

    for step in range(1, ns):
        greet(ti, lax.rem(si + step, ns))
    greet(chip * 2 + 1 - core, si)
    for step in range(1, chips):
        greet(lax.rem(ti + 2 * step, nt), si)

    def fetch(at, src, dst):
        return pltpu.make_async_copy(src, dst, in_sem.at[at])

    loads = [
        fetch(0, index_hbm, index_ref),
        fetch(1, label_hbm, label_ref),
        fetch(2, dual_hbm, dbuf.at[si]),
        fetch(3, support_hbm, support_ref),
    ] + [fetch(4 + c, pool_hbm.at[c], pool_refs[c]) for c in range(CHANNELS)]
    for at in (0, 4, 5, 6, 3, 2, 1):
        loads[at].start()

    def plane_copy(source_chip, gl, target_chip):
        part = tbuf.at[source_chip * 2 + core, gl]
        return pltpu.make_async_remote_copy(
            src_ref=part,
            dst_ref=part,
            send_sem=plane_send,
            recv_sem=plane_recv.at[source_chip, gl],
            device_id=(target_chip * 2 + core, si),
            device_id_type=MESH,
        )

    def swap_copy(source_chip, gl):
        part = tbuf.at[source_chip * 2 + core, gl]
        return pltpu.make_async_remote_copy(
            src_ref=part,
            dst_ref=part,
            send_sem=swap_send,
            recv_sem=plane_recv.at[source_chip, gl],
            device_id=(ti, beside),
            device_id_type=MESH,
        )

    def part_copy(source_chip, gl, side):
        part = tbuf.at[source_chip * 2 + side, gl]
        return pltpu.make_async_remote_copy(
            src_ref=part,
            dst_ref=part,
            send_sem=part_send,
            recv_sem=part_recv.at[source_chip, gl],
            device_id=(chip * 2 + 1 - core, si),
            device_id_type=MESH,
        )

    def dual_copy(s):
        return pltpu.make_async_remote_copy(
            src_ref=dbuf.at[si],
            dst_ref=dbuf.at[si],
            send_sem=dual_send,
            recv_sem=dual_recv,
            device_id=(ti, s),
            device_id_type=MESH,
        )

    def dual_all():
        slots = dbuf.at[pl.ds(0, ns - 1)]
        return pltpu.make_async_remote_copy(
            src_ref=slots,
            dst_ref=slots,
            send_sem=dual_send,
            recv_sem=dual_recv,
            device_id=(ti, lax.rem(si + 1, ns)),
            device_id_type=MESH,
        )

    def label_copy(t):
        return pltpu.make_async_remote_copy(
            src_ref=lbuf.at[ti],
            dst_ref=lbuf.at[ti],
            send_sem=label_send,
            recv_sem=label_recv,
            device_id=(t, si),
            device_id_type=MESH,
        )

    def label_all():
        slots = lbuf.at[pl.ds(0, nt - 1)]
        return pltpu.make_async_remote_copy(
            src_ref=slots,
            dst_ref=slots,
            send_sem=label_send,
            recv_sem=label_recv,
            device_id=(chip * 2 + 1 - core, si),
            device_id_type=MESH,
        )

    def k_copy(t, s):
        return pltpu.make_async_remote_copy(
            src_ref=kbuf.at[me],
            dst_ref=kbuf.at[me],
            send_sem=k_send,
            recv_sem=k_recv,
            device_id=(t, s),
            device_id_type=MESH,
        )

    def k_all():
        others_slots = kbuf.at[pl.ds(0, ndev - 1)]
        return pltpu.make_async_remote_copy(
            src_ref=others_slots,
            dst_ref=others_slots,
            send_sem=k_send,
            recv_sem=k_recv,
            device_id=(1 - core + chip * 2, si),
            device_id_type=MESH,
        )

    band_row = lax.broadcasted_iota(jnp.int32, (LANES, LANES), 0)
    band_col = lax.broadcasted_iota(jnp.int32, (LANES, LANES), 1)
    near = (jnp.abs(band_row - band_col) <= 1) & (band_row // SIDE == band_col // SIDE)
    near = jnp.where(near, 1.0, 0.0).astype(jnp.bfloat16)
    for part in range(2):
        band[pl.ds(part * LANES, LANES), :] = near
    wide_row = lax.broadcasted_iota(jnp.int32, (LANES, targets), 0)
    wide_col = lax.broadcasted_iota(jnp.int32, (LANES, targets), 1)
    into = jnp.where(wide_col % PACK == wide_row // SIDE, 1.0, 0.0).astype(jnp.bfloat16)
    tall_row = lax.broadcasted_iota(jnp.int32, (targets, LANES), 0)
    tall_col = lax.broadcasted_iota(jnp.int32, (targets, LANES), 1)
    onto = jnp.where(tall_row % PACK == tall_col // SIDE, 1.0, 0.0).astype(jnp.bfloat16)
    for part in range(3):
        gathers[pl.ds(part * LANES, LANES), :] = into
        spread[pl.ds(part * targets, targets), :] = onto
    keep_g = lax.broadcasted_iota(jnp.int32, (groups, targets), 0)
    keep_t = lax.broadcasted_iota(jnp.int32, (groups, targets), 1)
    keep[...] = jnp.where(keep_t // PACK == keep_g, 1.0, 0.0).astype(jnp.float32)
    pool = pool_hbm.shape[1] * SUB
    def choice(h):
        return lax.rem(si + h, groups_own)

    def take_group(gl):
        picks = [lax.rem(index_ref[gl * PACK + i], pool) for i in range(PACK)]
        for channel in range(CHANNELS):
            natural = [
                pool_refs[channel][at // SUB, :, pl.ds(at % SUB, 1), :].reshape(SUB, LANES)
                for at in picks
            ]
            phases = interleave(natural, mask)
            for k in range(PACK):
                tbuf[ti, gl, channel * PACK + k] = phases[k]

    loads[0].wait()
    for channel in range(CHANNELS):
        loads[4 + channel].wait()
    for h in range(0, groups_own, share):
        take_group(choice(h))

    pl.semaphore_wait(barrier, ns + chips - 1)

    def each_plane(action):
        for h in range(0, groups_own, share):
            for step in range(chips - 1, 0, -1):
                for target in (chip + step, chip - step):
                    pl.when((target >= 0) & (target < chips))(
                        functools.partial(action, choice(h), target)
                    )

    each_plane(lambda gl, target: plane_copy(chip, gl, target).start())
    for h in range(0, groups_own, share):
        part_copy(chip, choice(h), core).start()
    if share == 2:
        for h in range(1, groups_own, share):
            take_group(choice(h))
            part_copy(chip, choice(h), core).start()

    loads[2].wait()

    def send_dual(step, carry):
        dual_copy(lax.rem(si + step, ns)).start()
        return carry

    lax.fori_loop(1, ns, send_dual, 0)

    loads[3].wait()
    for m in range(own_s):
        reps = []
        for channel in range(CHANNELS):
            phases = replicate(support_ref[channel, :, m, :], mask)
            reps.append(phases)
            for k in range(PACK):
                srep[channel, k, m] = phases[k] * (1.0 / (9.0 * CHANNELS))
        levels = levels_of(reps, mask)
        for layer in range(LAYERS):
            for k in range(PACK):
                inverse = lax.rsqrt(levels[layer][k])
                sroot[layer, 0, k, m] = inverse * (STRETCH / 9.0**layer)
                sroot[layer, 1, k, m] = levels[layer][k] * inverse * (9.0**layer / (STRETCH * math.pi))
                shalf[layer, k, m] = inverse * (9.0 * CHANNELS / (STRETCH * math.pi))

    def layer_map(g, layer, cross, inverse, root):
        mapped = []
        for k in range(PACK):
            x = cross[k] * (inverse[k][None] * sroot[layer, 0, k])
            size = jnp.abs(x) if layer == 0 else x
            gap = jnp.maximum(STRETCH - size, 1e-20)
            rest = STRETCH + size
            half = gap * lax.rsqrt(gap)
            poly = size + MONIC[-1]
            for term in MONIC[-2::-1]:
                poly = poly * size + term
            bend = half * poly
            slope = jnp.where(x >= 0.0, 1.0 + bend, 0.0 - bend) if layer == 0 else 1.0 + bend
            sine = half * (rest * lax.rsqrt(rest))
            scaled = sine * root[k][None]
            amp[g, layer, k] = scaled
            ang[g, layer, k] = slope
            mapped.append(scaled * sroot[layer, 1, k] + slope * cross[k])
        return mapped

    def next_cross(mapped, layer):
        return [v + BETA * 9.0**layer for v in band_sum(mapped, mask, band)]

    def finish_group(g, at, j):
        cross = [v + BETA * 9.0 for v in across([mid[j, k] for k in range(PACK)], band)]
        for layer in range(1, LAYERS):
            inverse = [tlev[at, j, layer - 1, 0, k] for k in range(PACK)]
            root = [tlev[at, j, layer - 1, 1, k] for k in range(PACK)]
            mapped = layer_map(g, layer, cross, inverse, root)
            if layer + 1 < LAYERS:
                cross = next_cross(mapped, layer + 1)
        total = (mapped[0] + mapped[1]) + (mapped[2] + mapped[3])
        ksum[:, pl.ds(g, 1), :] = jnp.sum(total, axis=1, keepdims=True)

    def begin_group(owner, gl, at, j):
        g = owner * groups_own + gl
        image = [
            [tbuf[owner, gl, channel * PACK + k] for k in range(PACK)]
            for channel in range(CHANNELS)
        ]
        levels = levels_of(image, mask)
        inverse = [[lax.rsqrt(levels[layer][k]) for k in range(PACK)] for layer in range(LAYERS)]
        root = [
            [levels[layer][k] * inverse[layer][k] for k in range(PACK)] for layer in range(LAYERS)
        ]
        for layer in range(1, LAYERS):
            for k in range(PACK):
                tlev[at, j, layer - 1, 0, k] = inverse[layer][k]
                tlev[at, j, layer - 1, 1, k] = root[layer][k]
        current = []
        for k in range(PACK):
            total = image[0][k][None] * srep[0, k]
            for channel in range(1, CHANNELS):
                total = total + image[channel][k][None] * srep[channel, k]
            current.append(total)
        cross = [v + BETA for v in band_sum(current, mask, band)]
        summed = vertical(layer_map(g, 0, cross, inverse[0], root[0]), mask)
        for k in range(PACK):
            mid[j, k] = summed[k]

    def order(n):
        both = jnp.minimum(chip, chips - 1 - chip)
        h = (n + 1) // 2
        two_sided = jnp.where(n % 2 == 1, chip - h, chip + h)
        far = n - both
        one_sided = jnp.where(chip <= chips - 1 - chip, chip + far, chip - far)
        return jnp.where(n <= 2 * both, two_sided, one_sided)

    def block(before, old, at, fresh):
        for j, g in enumerate(before):
            finish_group(g, old, j)
        for j, (owner, gl) in enumerate(fresh):
            begin_group(owner, gl, at, j)
        return tuple(owner * groups_own + gl for owner, gl in fresh)

    def near_item(n, gl, direct):
        p = order(n)
        plane_copy(p, gl, chip).wait_recv()
        if share == 2:
            pl.when(direct)(lambda: swap_copy(p, gl).start())
        part_copy(p, gl, core).start()
        return p * 2 + core, gl

    def far_item(n, gl):
        p = order(n)
        part_copy(p, gl, 1 - core).wait_recv()
        return p * 2 + 1 - core, gl

    slots = max(chips - 1, 1)
    before = ()
    last = slots - 1
    own = [(side, h) for side in (0, 1) for h in range(groups_own)]
    for first in range(0, len(own), 2):
        fresh = [
            far_item(0, choice(h)) if side else (ti, choice(h))
            for side, h in own[first : first + 2]
        ]
        at = (first // 2 - groups_own) % slots
        before = block(before, last, at, fresh)
        last = at

    def sweep(h, before):
        gl = choice(h)
        direct = h % 2 == 0
        items = [(side, n) for side in (0, 1) for n in range(1, chips)]
        for first in range(0, len(items), 2):
            fresh = [
                far_item(n, gl) if side else near_item(n, gl, direct)
                for side, n in items[first : first + 2]
            ]
            at = first // 2
            before = block(before, (at - 1) % slots, at, fresh)
        return before

    before = lax.fori_loop(0, groups_own, sweep, before)
    block(before, slots - 1, 0, [])

    nt_dims = (((1,), (1,)), ((), ()))
    lane_sums = jnp.dot(
        split_rows(ksum[...].reshape(own_s * groups, LANES)), gathers[...],
        preferred_element_type=jnp.float32,
    ) * (1.0 / (PIXELS * 9.0 ** (LAYERS - 1)))
    picked = jnp.sum(lane_sums.reshape(own_s, groups, targets) * keep[...][None], axis=1)
    kbuf[me] = picked

    for dt in sorted(range(nt), key=lambda d: -min(d, nt - d)):
        for ds in range(ns - 1, -1, -1):
            if dt or ds:
                k_copy(lax.rem(ti + dt, nt), lax.rem(si + ds, ns)).start()

    loads[1].wait()
    row = lax.broadcasted_iota(jnp.int32, (SUB, LANES), 0)
    lane = lax.broadcasted_iota(jnp.int32, (SUB, LANES), 1)
    line = lax.broadcasted_iota(jnp.int32, (1, LANES), 1)
    label = jnp.zeros((SUB, LANES), jnp.int32)
    labels = jnp.zeros((1, LANES), jnp.int32)
    for r in range(own_t):
        value = label_ref[r]
        label = jnp.where(row == r, value, label)
        labels = jnp.where(line == ti * own_t + r, value, labels)
    own_onehot = jnp.where(label == lane, 1.0, 0.0).astype(jnp.float32)
    lbuf[ti] = labels

    def send_label(step, carry):
        label_copy(lax.rem(ti + step, nt)).start()
        return carry

    lax.fori_loop(1, nt, send_label, 0)

    held[...] = jnp.zeros_like(held)

    def pair_unit(step, carry):
        levels = across([held[0, at, k] for at in range(LAYERS) for k in range(PACK)], band)
        passes = across([held[1, at, k] for at in range(LAYERS) for k in range(PACK)], band)

        g = jnp.clip(step - LAYERS, 0, groups - 1)
        owner = g // groups_own
        gl = g % groups_own
        last = (LAYERS - 1) * PACK
        for channel in range(CHANNELS):
            for k in range(PACK):
                image = tbuf[owner, gl, channel * PACK + k]
                unit[g, channel, k] = (
                    passes[last + k] * image[None] + srep[channel, k] * levels[last + k]
                )
        for at in range(LAYERS - 1, -1, -1):
            g = jnp.clip(step - at, 0, groups - 1)
            layer = LAYERS - 1 - at
            term = [amp[g, layer, k] * shalf[layer, k] for k in range(PACK)]
            slope = [ang[g, layer, k] for k in range(PACK)]
            if at > 0:
                start = (at - 1) * PACK
                term = [t * passes[start + k] + levels[start + k] for k, t in enumerate(term)]
                slope = [v * passes[start + k] for k, v in enumerate(slope)]
            for k, v in enumerate(vertical(term, mask)):
                held[0, at, k] = v
            for k, v in enumerate(vertical(slope, mask)):
                held[1, at, k] = v
        return carry

    lax.fori_loop(0, groups + LAYERS, pair_unit, 0)

    dual_all().wait_recv()
    duals = dbuf[...].reshape(ns * dual_hbm.shape[0], CLASSES)
    own_duals = dbuf[si, pl.ds(ti * own_s, own_s), :]
    gram = lax.dot_general(
        own_duals, duals, nt_dims, precision=HIGH, preferred_element_type=jnp.float32
    )
    label_all().wait_recv()
    named = lbuf[0]
    for t in range(1, nt):
        named = named + lbuf[t]
    classes = lax.broadcasted_iota(jnp.int32, (CLASSES, targets), 0)
    onehot = jnp.where(classes == named[:, :targets], 1.0, 0.0).astype(jnp.float32)
    offset = jnp.dot(own_duals, onehot, precision=HIGH, preferred_element_type=jnp.float32)

    def sent(sem, count, width):
        part = tbuf.at[pl.ds(0, count), pl.ds(0, width)]
        pltpu.make_async_remote_copy(
            src_ref=part,
            dst_ref=part,
            send_sem=sem,
            recv_sem=plane_recv.at[chip, 0],
            device_id=(chip * 2 + 1 - core, si),
            device_id_type=MESH,
        ).wait_send()

    sent(plane_send, chips - 1, groups_own // share)
    if share == 2:
        sent(swap_send, chips - 1, groups_own // share)
    sent(part_send, chips, groups_own)
    dual_all().wait_send()
    label_all().wait_send()
    k_all().wait_send()

    k_all().wait_recv()
    columns = jnp.concatenate([kbuf[d] for d in range(ndev)], axis=0)
    weight = jnp.dot(gram, columns, precision=HIGH, preferred_element_type=jnp.float32) - offset
    weight = weight * (1.0 / (CHANNELS * 9.0**LAYERS))
    wide = (weight[:, None, :] * keep[...][None]).reshape(own_s * groups, targets)
    wexp[...] = jnp.dot(split_rows(wide), spread[...], preferred_element_type=jnp.float32)
    pred[...] = columns.T

    even = mask[4] % 2 == 0
    early = mask[4] < 2
    for m in range(own_s):
        sums = [[None] * PACK for _ in range(CHANNELS)]
        for g in range(groups):
            w = wexp[pl.ds(m * groups + g, SUB, stride=0), :]
            for channel in range(CHANNELS):
                for k in range(PACK):
                    value = w * unit[g, channel, k, m]
                    sums[channel][k] = value if g == 0 else sums[channel][k] + value
        for channel in range(CHANNELS):
            low = fold(sums[channel][0], sums[channel][1], even, SIDE)
            high = fold(sums[channel][2], sums[channel][3], even, SIDE)
            flat[channel, m] = fold(low, high, early, 2 * SIDE)
    residual_ref[...] = jnp.dot(
        pred[pl.ds(ti * own_t, own_t), :], duals, precision=HIGH, preferred_element_type=jnp.float32
    ) - own_onehot[:own_t, :CLASSES]
    for channel in range(CHANNELS):
        for s in range(SUB):
            grad_ref[channel, s] = flat[channel, :, s, :]


def hand_over(residual_ref, grad_ref, residual_out, grad_out):
    residual_out[...] = residual_ref[...]
    grad_out[...] = grad_ref[...]


def shards(nt, ns, target_pool, target_index, target_labels, dual_weights, support_images):
    own_t = target_index.shape[0]
    own_s = support_images.shape[0]
    groups_own = own_t // PACK
    groups = nt * groups_own
    chips = nt // 2
    ndev = nt * ns
    f32 = jnp.float32
    vmem = pl.BlockSpec(memory_space=pltpu.VMEM)
    hbm = pl.BlockSpec(memory_space=pltpu.HBM)
    dma = pltpu.SemaphoreType.DMA
    tile = (SUB, LANES)
    pool = target_pool.reshape(-1, SUB, CHANNELS, SUB, LANES).transpose(2, 0, 3, 1, 4)
    support = support_images.reshape(own_s, CHANNELS, SUB, LANES).transpose(1, 2, 0, 3)
    residual, grad = pl.pallas_call(
        functools.partial(kernel, nt, ns, own_t, own_s),
        out_shape=(
            jax.ShapeDtypeStruct((own_t, CLASSES), f32),
            jax.ShapeDtypeStruct((CHANNELS, SUB, own_s, LANES), f32),
        ),
        in_specs=[hbm] * 5,
        out_specs=(vmem, vmem),
        scratch_shapes=[
            pltpu.SMEM((own_t,), jnp.int32),
            pltpu.SMEM((own_t,), jnp.int32),
            *[pltpu.VMEM(pool.shape[1:], f32)] * CHANNELS,
            pltpu.VMEM(support.shape, f32),
            pltpu.VMEM((nt, groups_own, CHANNELS * PACK) + tile, f32),
            pltpu.VMEM((ns,) + dual_weights.shape, f32),
            pltpu.VMEM((nt, 1, LANES), jnp.int32),
            pltpu.VMEM((ndev, own_s, nt * own_t), f32),
            pltpu.VMEM((2 * LANES, LANES), jnp.bfloat16),
            pltpu.VMEM((3 * LANES, nt * own_t), jnp.bfloat16),
            pltpu.VMEM((3 * nt * own_t, LANES), jnp.bfloat16),
            pltpu.VMEM((groups, nt * own_t), f32),
            pltpu.VMEM((CHANNELS, PACK, own_s) + tile, f32),
            pltpu.VMEM((LAYERS, 2, PACK, own_s) + tile, f32),
            pltpu.VMEM((LAYERS, PACK, own_s) + tile, f32),
            pltpu.VMEM((max(chips - 1, 1), 2, LAYERS - 1, 2, PACK) + tile, f32),
            pltpu.VMEM((2, PACK, own_s) + tile, f32),
            pltpu.VMEM((2, LAYERS, PACK, own_s) + tile, f32),
            pltpu.VMEM((groups, LAYERS, PACK, own_s) + tile, f32),
            pltpu.VMEM((groups, LAYERS, PACK, own_s) + tile, f32),
            pltpu.VMEM((groups, CHANNELS, PACK, own_s) + tile, f32),
            pltpu.VMEM((own_s, groups, LANES), f32),
            pltpu.VMEM((own_s * groups, LANES), f32),
            pltpu.VMEM((nt * own_t, ns * dual_weights.shape[0]), f32),
            pltpu.VMEM((CHANNELS, own_s) + tile, f32),
            dma((4 + CHANNELS,)),
            dma,
            dma((chips, groups_own)),
            dma,
            dma,
            dma((chips, groups_own)),
            dma,
            dma,
            dma,
            dma,
            dma,
            dma,
        ],
        compiler_params=pltpu.CompilerParams(
            collective_id=0, has_side_effects=True, vmem_limit_bytes=44 * 2**20
        ),
    )(*[
        pltpu.with_memory_space_constraint(v, pltpu.HBM)
        for v in (target_index, target_labels, pool, dual_weights, support)
    ])
    residual, grad = pl.pallas_call(
        hand_over,
        out_shape=(
            jax.ShapeDtypeStruct(residual.shape, f32),
            jax.ShapeDtypeStruct(grad.shape, f32),
        ),
        in_specs=[vmem, vmem],
        out_specs=(vmem, vmem),
        compiler_params=pltpu.CompilerParams(vmem_limit_bytes=2**20),
    )(residual, grad)
    return (residual, grad.transpose(2, 0, 1, 3).reshape(support_images.shape))


def solution(mesh):
    in_specs = (
        P("tgt", None, None),
        P("tgt"),
        P("tgt"),
        P("sup", None),
        P(("sup", "tgt"), None, None),
    )
    out_specs = (P("tgt", None), P(("sup", "tgt"), None, None))
    body = functools.partial(shards, mesh.shape["tgt"], mesh.shape["sup"])
    return jax.shard_map(body, mesh=mesh, in_specs=in_specs, out_specs=out_specs, check_vma=False)
```

```python
import functools
import math

import jax
import jax.numpy as jnp
from jax import lax
from jax.experimental import pallas as pl
from jax.experimental.pallas import tpu as pltpu
from jax.sharding import PartitionSpec as P

CHANNELS = 3
SIDE = 32
CLASSES = 100
LAYERS = 3
PIXELS = 1024
BETA = 0.01
PACK = 4
SUB = 8
LANES = 128
MESH = pl.DeviceIdType.MESH
HIGH = lax.Precision.HIGHEST
ACOS = (
    1.5707956895,
    -0.2145428158,
    0.0881710453,
    -0.0459272047,
    0.0206200335,
    -0.0049111629,
)


STRETCH = (-ACOS[-1] / math.pi) ** (2.0 / (2 * len(ACOS) - 1))
MONIC = [
    term / ACOS[-1] * STRETCH ** (len(ACOS) - 1 - power) for power, term in enumerate(ACOS)
][:-1]


def masks():
    lane = lax.broadcasted_iota(jnp.int32, (SUB, LANES), 1)
    row = lax.broadcasted_iota(jnp.int32, (SUB, LANES), 0)
    column = lane % SIDE
    return (column > 0, column < SIDE - 1, row > 0, row < SUB - 1, lane // SIDE)


def box_sum(maps, mask):
    right, left, down, up, _ = mask
    axis = maps[0].ndim - 1

    def across(v):
        return (
            v
            + jnp.where(right, pltpu.roll(v, 1, axis), 0.0)
            + jnp.where(left, pltpu.roll(v, LANES - 1, axis), 0.0)
        )

    before = jnp.where(down, pltpu.roll(maps[3], 1, axis - 1), 0.0)
    after = jnp.where(up, pltpu.roll(maps[0], SUB - 1, axis - 1), 0.0)
    low = maps[0] + maps[1]
    high = maps[2] + maps[3]
    return [across(v) for v in (before + low, low + maps[2], maps[1] + high, high + after)]


def vertical(maps, mask):
    down, up = mask[2], mask[3]
    axis = maps[0].ndim - 2
    before = jnp.where(down, pltpu.roll(maps[3], 1, axis), 0.0)
    after = jnp.where(up, pltpu.roll(maps[0], SUB - 1, axis), 0.0)
    low = maps[0] + maps[1]
    high = maps[2] + maps[3]
    return [before + low, low + maps[2], maps[1] + high, high + after]


def band_sum(maps, mask, band):
    return across(vertical(maps, mask), band)


def across(maps, band):
    shape = maps[0].shape
    rows = jnp.stack(maps).reshape(-1, LANES)
    high = rows.astype(jnp.bfloat16)
    low = (rows - high.astype(jnp.float32)).astype(jnp.bfloat16)
    out = jnp.dot(
        jnp.concatenate([high, low], axis=1), band[...], preferred_element_type=jnp.float32
    ).reshape((len(maps),) + shape)
    return [out[k] for k in range(len(maps))]


def interleave(images, mask):
    group = mask[4]
    out = []
    for k in range(PACK):
        total = None
        for m in range(PACK):
            shift = ((m - k) * SIDE) % LANES
            moved = images[m] if shift == 0 else pltpu.roll(images[m], shift, 1)
            total = moved if total is None else jnp.where(group == m, moved, total)
        out.append(total)
    return out


def replicate(image, mask):
    group = mask[4]
    out = []
    rolled = [image] + [pltpu.roll(image, SIDE * s, 1) for s in range(1, PACK)]
    for k in range(PACK):
        total = None
        for m in range(PACK):
            moved = rolled[(m - k) % PACK]
            total = moved if total is None else jnp.where(group == m, moved, total)
        out.append(total)
    return out


def levels_of(images, mask):
    energy = []
    for k in range(PACK):
        total = images[0][k] * images[0][k]
        for channel in range(1, CHANNELS):
            total = total + images[channel][k] * images[channel][k]
        energy.append(total * (1.0 / CHANNELS))
    levels = []
    current = energy
    for _ in range(LAYERS):
        current = [v * (1.0 / 9.0) + BETA for v in box_sum(current, mask)]
        levels.append(current)
    return levels


def sharing(targets, own_s):
    per = max(LANES // targets, 1)
    return per if LANES % targets == 0 and own_s % per == 0 else 1


def split_rows(v):
    high = v.astype(jnp.bfloat16)
    rest = v - high.astype(jnp.float32)
    middle = rest.astype(jnp.bfloat16)
    low = (rest - middle.astype(jnp.float32)).astype(jnp.bfloat16)
    return jnp.concatenate([high, middle, low], axis=1)


def fold(a, b, keep, shift):
    return jnp.where(keep, a, b) + pltpu.roll(jnp.where(keep, b, a), shift, a.ndim - 1)


def kernel(
    nt, ns, own_t, own_s,
    index_hbm, label_hbm, pool_hbm, dual_hbm, support_hbm,
    residual_ref, grad_ref,
    index_ref, label_ref, pool_a, pool_b, pool_c, support_ref,
    tbuf, dbuf, lbuf, kbuf, band, gathers, spread, keep, srep, sroot, shalf, tlev, mid, held, amp, ang, unit, ksum, wexp, pred, flat,
    in_sem, plane_send, plane_recv, swap_send, part_send, part_recv,
    dual_send, dual_recv, label_send, label_recv, k_send, k_recv,
):
    ti = lax.axis_index("tgt")
    si = lax.axis_index("sup")
    pool_refs = (pool_a, pool_b, pool_c)
    chips = nt // 2
    chip = ti // 2
    core = ti % 2
    ndev = nt * ns
    me = si * nt + ti
    groups_own = own_t // PACK
    groups = nt * groups_own
    targets = nt * own_t
    per = sharing(targets, own_s)
    mask = masks()
    share = 2 if groups_own % 2 == 0 and ns % 2 == 0 else 1
    beside = si + 1 - 2 * (si % 2)
    barrier = pltpu.get_barrier_semaphore()

    def greet(t, s):
        pl.semaphore_signal(barrier, inc=1, device_id=(t, s), device_id_type=MESH)

    for step in range(1, ns):
        greet(ti, lax.rem(si + step, ns))
    greet(chip * 2 + 1 - core, si)
    for step in range(1, chips):
        greet(lax.rem(ti + 2 * step, nt), si)

    def fetch(at, src, dst):
        return pltpu.make_async_copy(src, dst, in_sem.at[at])

    loads = [
        fetch(0, index_hbm, index_ref),
        fetch(1, label_hbm, label_ref),
        fetch(2, dual_hbm, dbuf.at[si]),
        fetch(3, support_hbm, support_ref),
    ] + [fetch(4 + c, pool_hbm.at[c], pool_refs[c]) for c in range(CHANNELS)]
    for at in (0, 4, 5, 6, 3, 2, 1):
        loads[at].start()

    def plane_copy(source_chip, gl, target_chip):
        part = tbuf.at[source_chip * 2 + core, gl]
        return pltpu.make_async_remote_copy(
            src_ref=part,
            dst_ref=part,
            send_sem=plane_send,
            recv_sem=plane_recv.at[source_chip, gl],
            device_id=(target_chip * 2 + core, si),
            device_id_type=MESH,
        )

    def swap_copy(source_chip, gl):
        part = tbuf.at[source_chip * 2 + core, gl]
        return pltpu.make_async_remote_copy(
            src_ref=part,
            dst_ref=part,
            send_sem=swap_send,
            recv_sem=plane_recv.at[source_chip, gl],
            device_id=(ti, beside),
            device_id_type=MESH,
        )

    def part_copy(source_chip, gl, side):
        part = tbuf.at[source_chip * 2 + side, gl]
        return pltpu.make_async_remote_copy(
            src_ref=part,
            dst_ref=part,
            send_sem=part_send,
            recv_sem=part_recv.at[source_chip, gl],
            device_id=(chip * 2 + 1 - core, si),
            device_id_type=MESH,
        )

    def dual_copy(s):
        return pltpu.make_async_remote_copy(
            src_ref=dbuf.at[si],
            dst_ref=dbuf.at[si],
            send_sem=dual_send,
            recv_sem=dual_recv,
            device_id=(ti, s),
            device_id_type=MESH,
        )

    def dual_all():
        slots = dbuf.at[pl.ds(0, ns - 1)]
        return pltpu.make_async_remote_copy(
            src_ref=slots,
            dst_ref=slots,
            send_sem=dual_send,
            recv_sem=dual_recv,
            device_id=(ti, lax.rem(si + 1, ns)),
            device_id_type=MESH,
        )

    def label_copy(t):
        return pltpu.make_async_remote_copy(
            src_ref=lbuf.at[ti],
            dst_ref=lbuf.at[ti],
            send_sem=label_send,
            recv_sem=label_recv,
            device_id=(t, si),
            device_id_type=MESH,
        )

    def label_all():
        slots = lbuf.at[pl.ds(0, nt - 1)]
        return pltpu.make_async_remote_copy(
            src_ref=slots,
            dst_ref=slots,
            send_sem=label_send,
            recv_sem=label_recv,
            device_id=(chip * 2 + 1 - core, si),
            device_id_type=MESH,
        )

    def k_copy(t, s):
        return pltpu.make_async_remote_copy(
            src_ref=kbuf.at[me],
            dst_ref=kbuf.at[me],
            send_sem=k_send,
            recv_sem=k_recv,
            device_id=(t, s),
            device_id_type=MESH,
        )

    def k_all():
        others_slots = kbuf.at[pl.ds(0, ndev - 1)]
        return pltpu.make_async_remote_copy(
            src_ref=others_slots,
            dst_ref=others_slots,
            send_sem=k_send,
            recv_sem=k_recv,
            device_id=(1 - core + chip * 2, si),
            device_id_type=MESH,
        )

    band_row = lax.broadcasted_iota(jnp.int32, (LANES, LANES), 0)
    band_col = lax.broadcasted_iota(jnp.int32, (LANES, LANES), 1)
    near = (jnp.abs(band_row - band_col) <= 1) & (band_row // SIDE == band_col // SIDE)
    near = jnp.where(near, 1.0, 0.0).astype(jnp.bfloat16)
    for part in range(2):
        band[pl.ds(part * LANES, LANES), :] = near
    wide_row = lax.broadcasted_iota(jnp.int32, (LANES, per * targets), 0)
    wide_col = lax.broadcasted_iota(jnp.int32, (LANES, per * targets), 1)
    into = jnp.where(wide_col % PACK == wide_row // SIDE, 1.0, 0.0).astype(jnp.bfloat16)
    tall_row = lax.broadcasted_iota(jnp.int32, (targets, LANES), 0)
    tall_col = lax.broadcasted_iota(jnp.int32, (targets, LANES), 1)
    onto = jnp.where(tall_row % PACK == tall_col // SIDE, 1.0, 0.0).astype(jnp.bfloat16)
    for part in range(3):
        gathers[pl.ds(part * LANES, LANES), :] = into
        spread[pl.ds(part * targets, targets), :] = onto
    keep_g = lax.broadcasted_iota(jnp.int32, (groups, per * targets), 0)
    keep_t = lax.broadcasted_iota(jnp.int32, (groups, per * targets), 1)
    keep[...] = jnp.where(keep_t % targets // PACK == keep_g, 1.0, 0.0).astype(jnp.float32)
    pool = pool_hbm.shape[1] * SUB
    def choice(h):
        return lax.rem(si + h, groups_own)

    def take_group(gl):
        picks = [lax.rem(index_ref[gl * PACK + i], pool) for i in range(PACK)]
        for channel in range(CHANNELS):
            natural = [
                pool_refs[channel][at // SUB, :, pl.ds(at % SUB, 1), :].reshape(SUB, LANES)
                for at in picks
            ]
            phases = interleave(natural, mask)
            for k in range(PACK):
                tbuf[ti, gl, channel * PACK + k] = phases[k]

    loads[0].wait()
    for channel in range(CHANNELS):
        loads[4 + channel].wait()
    for h in range(0, groups_own, share):
        take_group(choice(h))

    pl.semaphore_wait(barrier, ns + chips - 1)

    def each_plane(action):
        for h in range(0, groups_own, share):
            for step in range(chips - 1, 0, -1):
                for target in (chip + step, chip - step):
                    pl.when((target >= 0) & (target < chips))(
                        functools.partial(action, choice(h), target)
                    )

    each_plane(lambda gl, target: plane_copy(chip, gl, target).start())
    for h in range(0, groups_own, share):
        part_copy(chip, choice(h), core).start()
    if share == 2:
        for h in range(1, groups_own, share):
            take_group(choice(h))
            part_copy(chip, choice(h), core).start()

    loads[2].wait()

    def send_dual(step, carry):
        dual_copy(lax.rem(si + step, ns)).start()
        return carry

    lax.fori_loop(1, ns, send_dual, 0)

    loads[3].wait()
    for m in range(own_s):
        reps = []
        for channel in range(CHANNELS):
            phases = replicate(support_ref[channel, :, m, :], mask)
            reps.append(phases)
            for k in range(PACK):
                srep[channel, k, m] = phases[k] * (1.0 / (9.0 * CHANNELS))
        levels = levels_of(reps, mask)
        for layer in range(LAYERS):
            for k in range(PACK):
                inverse = lax.rsqrt(levels[layer][k])
                sroot[layer, 0, k, m] = inverse * (STRETCH / 9.0**layer)
                sroot[layer, 1, k, m] = levels[layer][k] * inverse * (9.0**layer / (STRETCH * math.pi))
                shalf[layer, k, m] = inverse * (9.0 * CHANNELS / (STRETCH * math.pi))

    def layer_map(g, layer, cross, inverse, root):
        mapped = []
        for k in range(PACK):
            x = cross[k] * (inverse[k][None] * sroot[layer, 0, k])
            size = jnp.abs(x) if layer == 0 else x
            gap = jnp.maximum(STRETCH - size, 1e-20)
            rest = STRETCH + size
            half = gap * lax.rsqrt(gap)
            poly = size + MONIC[-1]
            for term in MONIC[-2::-1]:
                poly = poly * size + term
            bend = half * poly
            slope = jnp.where(x >= 0.0, 1.0 + bend, 0.0 - bend) if layer == 0 else 1.0 + bend
            sine = half * (rest * lax.rsqrt(rest))
            scaled = sine * root[k][None]
            amp[g, layer, k] = scaled
            ang[g, layer, k] = slope
            mapped.append(scaled * sroot[layer, 1, k] + slope * cross[k])
        return mapped

    def next_cross(mapped, layer):
        return [v + BETA * 9.0**layer for v in band_sum(mapped, mask, band)]

    def finish_group(g, at, j):
        cross = [v + BETA * 9.0 for v in across([mid[j, k] for k in range(PACK)], band)]
        for layer in range(1, LAYERS):
            inverse = [tlev[at, j, layer - 1, 0, k] for k in range(PACK)]
            root = [tlev[at, j, layer - 1, 1, k] for k in range(PACK)]
            mapped = layer_map(g, layer, cross, inverse, root)
            if layer + 1 < LAYERS:
                cross = next_cross(mapped, layer + 1)
        total = (mapped[0] + mapped[1]) + (mapped[2] + mapped[3])
        ksum[:, pl.ds(g, 1), :] = jnp.sum(total, axis=1, keepdims=True)

    def begin_group(owner, gl, at, j):
        g = owner * groups_own + gl
        image = [
            [tbuf[owner, gl, channel * PACK + k] for k in range(PACK)]
            for channel in range(CHANNELS)
        ]
        levels = levels_of(image, mask)
        inverse = [[lax.rsqrt(levels[layer][k]) for k in range(PACK)] for layer in range(LAYERS)]
        root = [
            [levels[layer][k] * inverse[layer][k] for k in range(PACK)] for layer in range(LAYERS)
        ]
        for layer in range(1, LAYERS):
            for k in range(PACK):
                tlev[at, j, layer - 1, 0, k] = inverse[layer][k]
                tlev[at, j, layer - 1, 1, k] = root[layer][k]
        current = []
        for k in range(PACK):
            total = image[0][k][None] * srep[0, k]
            for channel in range(1, CHANNELS):
                total = total + image[channel][k][None] * srep[channel, k]
            current.append(total)
        cross = [v + BETA for v in band_sum(current, mask, band)]
        summed = vertical(layer_map(g, 0, cross, inverse[0], root[0]), mask)
        for k in range(PACK):
            mid[j, k] = summed[k]

    def order(n):
        both = jnp.minimum(chip, chips - 1 - chip)
        h = (n + 1) // 2
        two_sided = jnp.where(n % 2 == 1, chip - h, chip + h)
        far = n - both
        one_sided = jnp.where(chip <= chips - 1 - chip, chip + far, chip - far)
        return jnp.where(n <= 2 * both, two_sided, one_sided)

    def block(before, old, at, fresh):
        for j, g in enumerate(before):
            finish_group(g, old, j)
        for j, (owner, gl) in enumerate(fresh):
            begin_group(owner, gl, at, j)
        return tuple(owner * groups_own + gl for owner, gl in fresh)

    def near_item(n, gl, direct):
        p = order(n)
        plane_copy(p, gl, chip).wait_recv()
        if share == 2:
            pl.when(direct)(lambda: swap_copy(p, gl).start())
        part_copy(p, gl, core).start()
        return p * 2 + core, gl

    def far_item(n, gl):
        p = order(n)
        part_copy(p, gl, 1 - core).wait_recv()
        return p * 2 + 1 - core, gl

    slots = max(chips - 1, 1)
    before = ()
    last = slots - 1
    own = [(side, h) for side in (0, 1) for h in range(groups_own)]
    for first in range(0, len(own), 2):
        fresh = [
            far_item(0, choice(h)) if side else (ti, choice(h))
            for side, h in own[first : first + 2]
        ]
        at = (first // 2 - groups_own) % slots
        before = block(before, last, at, fresh)
        last = at

    def sweep(h, before):
        gl = choice(h)
        direct = h % 2 == 0
        items = [(side, n) for side in (0, 1) for n in range(1, chips)]
        for first in range(0, len(items), 2):
            fresh = [
                far_item(n, gl) if side else near_item(n, gl, direct)
                for side, n in items[first : first + 2]
            ]
            at = first // 2
            before = block(before, (at - 1) % slots, at, fresh)
        return before

    before = lax.fori_loop(0, groups_own, sweep, before)
    block(before, slots - 1, 0, [])

    nt_dims = (((1,), (1,)), ((), ()))
    lane_sums = jnp.dot(
        split_rows(ksum[...].reshape(own_s * groups, LANES)), gathers[...],
        preferred_element_type=jnp.float32,
    ) * (1.0 / (PIXELS * 9.0 ** (LAYERS - 1)))
    picked = jnp.sum(lane_sums.reshape(own_s, groups, per * targets) * keep[...][None], axis=1)
    half = lax.broadcasted_iota(jnp.int32, (1, per * targets), 1) // targets
    for r in range(own_s // per):
        packed = picked[r * per : r * per + 1]
        for h in range(1, per):
            packed = jnp.where(half == h, picked[r * per + h : r * per + h + 1], packed)
        kbuf[me, pl.ds(r, 1), :] = packed

    for dt in sorted(range(nt), key=lambda d: -min(d, nt - d)):
        for ds in range(ns - 1, -1, -1):
            if dt or ds:
                k_copy(lax.rem(ti + dt, nt), lax.rem(si + ds, ns)).start()

    loads[1].wait()
    row = lax.broadcasted_iota(jnp.int32, (SUB, LANES), 0)
    lane = lax.broadcasted_iota(jnp.int32, (SUB, LANES), 1)
    line = lax.broadcasted_iota(jnp.int32, (1, LANES), 1)
    label = jnp.zeros((SUB, LANES), jnp.int32)
    labels = jnp.zeros((1, LANES), jnp.int32)
    for r in range(own_t):
        value = label_ref[r]
        label = jnp.where(row == r, value, label)
        labels = jnp.where(line == ti * own_t + r, value, labels)
    own_onehot = jnp.where(label == lane, 1.0, 0.0).astype(jnp.float32)
    lbuf[ti] = labels

    def send_label(step, carry):
        label_copy(lax.rem(ti + step, nt)).start()
        return carry

    lax.fori_loop(1, nt, send_label, 0)

    def pair_step(step, stages):
        ready = [at - 1 for at in stages if at > 0]
        levels, passes = [
            dict(zip(
                [(at, k) for at in ready for k in range(PACK)],
                across([held[which, at, k] for at in ready for k in range(PACK)], band)
                if ready else [],
            ))
            for which in range(2)
        ]
        for at in sorted(stages, reverse=True):
            g = step - at
            if at == LAYERS:
                owner = g // groups_own
                gl = g % groups_own
                for channel in range(CHANNELS):
                    for k in range(PACK):
                        image = tbuf[owner, gl, channel * PACK + k]
                        unit[g, channel, k] = (
                            passes[at - 1, k] * image[None] + srep[channel, k] * levels[at - 1, k]
                        )
                continue
            layer = LAYERS - 1 - at
            term = [amp[g, layer, k] * shalf[layer, k] for k in range(PACK)]
            slope = [ang[g, layer, k] for k in range(PACK)]
            if at > 0:
                term = [t * passes[at - 1, k] + levels[at - 1, k] for k, t in enumerate(term)]
                slope = [v * passes[at - 1, k] for k, v in enumerate(slope)]
            for k, v in enumerate(vertical(term, mask)):
                held[0, at, k] = v
            for k, v in enumerate(vertical(slope, mask)):
                held[1, at, k] = v

    span = 2
    whole = max(groups - LAYERS, 0) // span

    def pair_unit(trip, carry):
        for extra in range(span):
            pair_step(LAYERS + trip * span + extra, range(LAYERS + 1))
        return carry

    for step in range(min(LAYERS, groups)):
        pair_step(step, range(step + 1))
    lax.fori_loop(0, whole, pair_unit, 0)
    for step in range(LAYERS + whole * span, groups):
        pair_step(step, range(LAYERS + 1))
    for step in range(groups, groups + LAYERS):
        pair_step(step, range(step - groups + 1, LAYERS + 1))

    dual_all().wait_recv()
    rows = dual_hbm.shape[0] // per

    def dual_rows(h):
        if per == 1:
            return dbuf[...].reshape(ns * rows, CLASSES)
        return jnp.concatenate([dbuf[s, pl.ds(h, rows, stride=per), :] for s in range(ns)], axis=0)

    own_duals = dbuf[si, pl.ds(ti * own_s, own_s), :]
    gram = jnp.concatenate(
        [
            lax.dot_general(
                own_duals, dual_rows(h), nt_dims, precision=HIGH, preferred_element_type=jnp.float32
            )
            for h in range(per)
        ],
        axis=0,
    )
    label_all().wait_recv()
    named = lbuf[0]
    for t in range(1, nt):
        named = named + lbuf[t]
    classes = lax.broadcasted_iota(jnp.int32, (CLASSES, targets), 0)
    onehot = jnp.where(classes == named[:, :targets], 1.0, 0.0).astype(jnp.float32)
    offset = jnp.dot(own_duals, onehot, precision=HIGH, preferred_element_type=jnp.float32)

    def sent(sem, count, width):
        part = tbuf.at[pl.ds(0, count), pl.ds(0, width)]
        pltpu.make_async_remote_copy(
            src_ref=part,
            dst_ref=part,
            send_sem=sem,
            recv_sem=plane_recv.at[chip, 0],
            device_id=(chip * 2 + 1 - core, si),
            device_id_type=MESH,
        ).wait_send()

    sent(plane_send, chips - 1, groups_own // share)
    if share == 2:
        sent(swap_send, chips - 1, groups_own // share)
    sent(part_send, chips, groups_own)
    dual_all().wait_send()
    label_all().wait_send()
    k_all().wait_send()

    k_all().wait_recv()
    columns = jnp.concatenate([kbuf[d] for d in range(ndev)], axis=0)
    both = jnp.dot(gram, columns, precision=HIGH, preferred_element_type=jnp.float32)
    weight = -offset
    for h in range(per):
        weight = weight + both[h * own_s : (h + 1) * own_s, h * targets : (h + 1) * targets]
    weight = weight * (1.0 / (CHANNELS * 9.0**LAYERS))
    wide = (weight[:, None, :] * keep[:, :targets][None]).reshape(own_s * groups, targets)
    wexp[...] = jnp.dot(split_rows(wide), spread[...], preferred_element_type=jnp.float32)
    pred[...] = columns.T

    even = mask[4] % 2 == 0
    early = mask[4] < 2
    for m in range(own_s):
        sums = [[None] * PACK for _ in range(CHANNELS)]
        for g in range(groups):
            w = wexp[pl.ds(m * groups + g, SUB, stride=0), :]
            for channel in range(CHANNELS):
                for k in range(PACK):
                    value = w * unit[g, channel, k, m]
                    sums[channel][k] = value if g == 0 else sums[channel][k] + value
        for channel in range(CHANNELS):
            low = fold(sums[channel][0], sums[channel][1], even, SIDE)
            high = fold(sums[channel][2], sums[channel][3], even, SIDE)
            flat[channel, m] = fold(low, high, early, 2 * SIDE)
    residual = -own_onehot[:own_t, :CLASSES]
    for h in range(per):
        residual = residual + jnp.dot(
            pred[pl.ds(h * targets + ti * own_t, own_t), :], dual_rows(h),
            precision=HIGH, preferred_element_type=jnp.float32,
        )
    residual_ref[...] = residual
    for channel in range(CHANNELS):
        for s in range(SUB):
            grad_ref[channel, s] = flat[channel, :, s, :]


def hand_over(residual_ref, grad_ref, residual_out, grad_out):
    residual_out[...] = residual_ref[...]
    grad_out[...] = grad_ref[...]


def shards(nt, ns, target_pool, target_index, target_labels, dual_weights, support_images):
    own_t = target_index.shape[0]
    own_s = support_images.shape[0]
    groups_own = own_t // PACK
    groups = nt * groups_own
    chips = nt // 2
    ndev = nt * ns
    per = sharing(nt * own_t, own_s)
    f32 = jnp.float32
    vmem = pl.BlockSpec(memory_space=pltpu.VMEM)
    hbm = pl.BlockSpec(memory_space=pltpu.HBM)
    dma = pltpu.SemaphoreType.DMA
    tile = (SUB, LANES)
    pool = target_pool.reshape(-1, SUB, CHANNELS, SUB, LANES).transpose(2, 0, 3, 1, 4)
    support = support_images.reshape(own_s, CHANNELS, SUB, LANES).transpose(1, 2, 0, 3)
    residual, grad = pl.pallas_call(
        functools.partial(kernel, nt, ns, own_t, own_s),
        out_shape=(
            jax.ShapeDtypeStruct((own_t, CLASSES), f32),
            jax.ShapeDtypeStruct((CHANNELS, SUB, own_s, LANES), f32),
        ),
        in_specs=[hbm] * 5,
        out_specs=(vmem, vmem),
        scratch_shapes=[
            pltpu.SMEM((own_t,), jnp.int32),
            pltpu.SMEM((own_t,), jnp.int32),
            *[pltpu.VMEM(pool.shape[1:], f32)] * CHANNELS,
            pltpu.VMEM(support.shape, f32),
            pltpu.VMEM((nt, groups_own, CHANNELS * PACK) + tile, f32),
            pltpu.VMEM((ns,) + dual_weights.shape, f32),
            pltpu.VMEM((nt, 1, LANES), jnp.int32),
            pltpu.VMEM((ndev, own_s // per, per * nt * own_t), f32),
            pltpu.VMEM((2 * LANES, LANES), jnp.bfloat16),
            pltpu.VMEM((3 * LANES, per * nt * own_t), jnp.bfloat16),
            pltpu.VMEM((3 * nt * own_t, LANES), jnp.bfloat16),
            pltpu.VMEM((groups, per * nt * own_t), f32),
            pltpu.VMEM((CHANNELS, PACK, own_s) + tile, f32),
            pltpu.VMEM((LAYERS, 2, PACK, own_s) + tile, f32),
            pltpu.VMEM((LAYERS, PACK, own_s) + tile, f32),
            pltpu.VMEM((max(chips - 1, 1), 2, LAYERS - 1, 2, PACK) + tile, f32),
            pltpu.VMEM((2, PACK, own_s) + tile, f32),
            pltpu.VMEM((2, LAYERS, PACK, own_s) + tile, f32),
            pltpu.VMEM((groups, LAYERS, PACK, own_s) + tile, f32),
            pltpu.VMEM((groups, LAYERS, PACK, own_s) + tile, f32),
            pltpu.VMEM((groups, CHANNELS, PACK, own_s) + tile, f32),
            pltpu.VMEM((own_s, groups, LANES), f32),
            pltpu.VMEM((own_s * groups, LANES), f32),
            pltpu.VMEM((per * nt * own_t, ns * dual_weights.shape[0] // per), f32),
            pltpu.VMEM((CHANNELS, own_s) + tile, f32),
            dma((4 + CHANNELS,)),
            dma,
            dma((chips, groups_own)),
            dma,
            dma,
            dma((chips, groups_own)),
            dma,
            dma,
            dma,
            dma,
            dma,
            dma,
        ],
        compiler_params=pltpu.CompilerParams(
            collective_id=0, has_side_effects=True, vmem_limit_bytes=44 * 2**20
        ),
    )(*[
        pltpu.with_memory_space_constraint(v, pltpu.HBM)
        for v in (target_index, target_labels, pool, dual_weights, support)
    ])
    residual, grad = pl.pallas_call(
        hand_over,
        out_shape=(
            jax.ShapeDtypeStruct(residual.shape, f32),
            jax.ShapeDtypeStruct(grad.shape, f32),
        ),
        in_specs=[vmem, vmem],
        out_specs=(vmem, vmem),
        compiler_params=pltpu.CompilerParams(vmem_limit_bytes=2**20),
    )(residual, grad)
    return (residual, grad.transpose(2, 0, 1, 3).reshape(support_images.shape))


def solution(mesh):
    in_specs = (
        P("tgt", None, None),
        P("tgt"),
        P("tgt"),
        P("sup", None),
        P(("sup", "tgt"), None, None),
    )
    out_specs = (P("tgt", None), P(("sup", "tgt"), None, None))
    body = functools.partial(shards, mesh.shape["tgt"], mesh.shape["sup"])
    return jax.shard_map(body, mesh=mesh, in_specs=in_specs, out_specs=out_specs, check_vma=False)
```

```python
import functools
import math

import jax
import jax.numpy as jnp
from jax import lax
from jax.experimental import pallas as pl
from jax.experimental.pallas import tpu as pltpu
from jax.sharding import PartitionSpec as P

CHANNELS = 3
SIDE = 32
CLASSES = 100
LAYERS = 3
PIXELS = 1024
BETA = 0.01
PACK = 4
SUB = 8
LANES = 128
MESH = pl.DeviceIdType.MESH
HIGH = lax.Precision.HIGHEST
ACOS = (
    1.5707956895,
    -0.2145428158,
    0.0881710453,
    -0.0459272047,
    0.0206200335,
    -0.0049111629,
)


STRETCH = (-ACOS[-1] / math.pi) ** (2.0 / (2 * len(ACOS) - 1))
MONIC = [
    term / ACOS[-1] * STRETCH ** (len(ACOS) - 1 - power) for power, term in enumerate(ACOS)
][:-1]


def masks():
    lane = lax.broadcasted_iota(jnp.int32, (SUB, LANES), 1)
    row = lax.broadcasted_iota(jnp.int32, (SUB, LANES), 0)
    column = lane % SIDE
    return (column > 0, column < SIDE - 1, row > 0, row < SUB - 1, lane // SIDE)


def box_sum(maps, mask):
    right, left, down, up, _ = mask
    axis = maps[0].ndim - 1

    def across(v):
        return (
            v
            + jnp.where(right, pltpu.roll(v, 1, axis), 0.0)
            + jnp.where(left, pltpu.roll(v, LANES - 1, axis), 0.0)
        )

    before = jnp.where(down, pltpu.roll(maps[3], 1, axis - 1), 0.0)
    after = jnp.where(up, pltpu.roll(maps[0], SUB - 1, axis - 1), 0.0)
    low = maps[0] + maps[1]
    high = maps[2] + maps[3]
    return [across(v) for v in (before + low, low + maps[2], maps[1] + high, high + after)]


def vertical(maps, mask):
    down, up = mask[2], mask[3]
    axis = maps[0].ndim - 2
    before = jnp.where(down, pltpu.roll(maps[3], 1, axis), 0.0)
    after = jnp.where(up, pltpu.roll(maps[0], SUB - 1, axis), 0.0)
    low = maps[0] + maps[1]
    high = maps[2] + maps[3]
    return [before + low, low + maps[2], maps[1] + high, high + after]


def band_sum(maps, mask, band):
    return across(vertical(maps, mask), band)


def across(maps, band):
    shape = maps[0].shape
    rows = jnp.stack(maps).reshape(-1, LANES)
    high = rows.astype(jnp.bfloat16)
    low = (rows - high.astype(jnp.float32)).astype(jnp.bfloat16)
    out = jnp.dot(
        jnp.concatenate([high, low], axis=1), band[...], preferred_element_type=jnp.float32
    ).reshape((len(maps),) + shape)
    return [out[k] for k in range(len(maps))]


def interleave(images, mask):
    group = mask[4]
    out = []
    for k in range(PACK):
        total = None
        for m in range(PACK):
            shift = ((m - k) * SIDE) % LANES
            moved = images[m] if shift == 0 else pltpu.roll(images[m], shift, 1)
            total = moved if total is None else jnp.where(group == m, moved, total)
        out.append(total)
    return out


def replicate(image, mask):
    group = mask[4]
    out = []
    rolled = [image] + [pltpu.roll(image, SIDE * s, 1) for s in range(1, PACK)]
    for k in range(PACK):
        total = None
        for m in range(PACK):
            moved = rolled[(m - k) % PACK]
            total = moved if total is None else jnp.where(group == m, moved, total)
        out.append(total)
    return out


def levels_of(images, mask):
    energy = []
    for k in range(PACK):
        total = images[0][k] * images[0][k]
        for channel in range(1, CHANNELS):
            total = total + images[channel][k] * images[channel][k]
        energy.append(total * (1.0 / CHANNELS))
    levels = []
    current = energy
    for _ in range(LAYERS):
        current = [v * (1.0 / 9.0) + BETA for v in box_sum(current, mask)]
        levels.append(current)
    return levels


def sharing(targets, own_s):
    per = max(LANES // targets, 1)
    return per if LANES % targets == 0 and own_s % per == 0 else 1


def split_parts(v):
    high = v.astype(jnp.bfloat16)
    rest = v - high.astype(jnp.float32)
    middle = rest.astype(jnp.bfloat16)
    return high, middle, (rest - middle.astype(jnp.float32)).astype(jnp.bfloat16)


def split_rows(v):
    return jnp.concatenate(split_parts(v), axis=1)


def fold(a, b, keep, shift):
    return jnp.where(keep, a, b) + pltpu.roll(jnp.where(keep, b, a), shift, a.ndim - 1)


def kernel(
    nt, ns, own_t, own_s,
    index_hbm, label_hbm, pool_hbm, dual_hbm, support_hbm,
    residual_ref, grad_ref,
    index_ref, label_ref, pool_a, pool_b, pool_c, support_ref,
    tbuf, dbuf, lbuf, kbuf, band, gathers, spread, keep, srep, sroot, shalf, tlev, mid, held, amp, ang, unit, ksum, wexp, pred, flat,
    in_sem, plane_send, plane_recv, swap_send, edge_send, part_send, part_recv,
    dual_send, dual_recv, label_send, label_recv, k_send, k_recv,
):
    ti = lax.axis_index("tgt")
    si = lax.axis_index("sup")
    pool_refs = (pool_a, pool_b, pool_c)
    chips = nt // 2
    chip = ti // 2
    core = ti % 2
    ndev = nt * ns
    me = si * nt + ti
    groups_own = own_t // PACK
    groups = nt * groups_own
    targets = nt * own_t
    per = sharing(targets, own_s)
    mask = masks()
    share = 2 if groups_own % 2 == 0 and ns % 2 == 0 else 1
    beside = si + 1 - 2 * (si % 2)
    barrier = pltpu.get_barrier_semaphore()

    def greet(t, s):
        pl.semaphore_signal(barrier, inc=1, device_id=(t, s), device_id_type=MESH)

    def fetch(at, src, dst):
        return pltpu.make_async_copy(src, dst, in_sem.at[at])

    loads = [
        fetch(0, index_hbm, index_ref),
        fetch(1, label_hbm, label_ref),
        fetch(2, dual_hbm, dbuf.at[si]),
        fetch(3, support_hbm, support_ref),
    ] + [fetch(4 + c, pool_hbm.at[c], pool_refs[c]) for c in range(CHANNELS)]
    for at in (0, 4, 5, 6):
        loads[at].start()

    for step in range(1, ns):
        greet(ti, lax.rem(si + step, ns))
    greet(chip * 2 + 1 - core, si)
    for step in range(1, chips):
        greet(lax.rem(ti + 2 * step, nt), si)

    for at in (3, 2, 1):
        loads[at].start()

    def plane_copy(source_chip, gl, target_chip):
        part = tbuf.at[source_chip * 2 + core, gl]
        return pltpu.make_async_remote_copy(
            src_ref=part,
            dst_ref=part,
            send_sem=plane_send,
            recv_sem=plane_recv.at[source_chip, gl],
            device_id=(target_chip * 2 + core, si),
            device_id_type=MESH,
        )

    def swap_copy(source_chip, gl):
        part = tbuf.at[source_chip * 2 + core, gl]
        return pltpu.make_async_remote_copy(
            src_ref=part,
            dst_ref=part,
            send_sem=swap_send,
            recv_sem=plane_recv.at[source_chip, gl],
            device_id=(ti, beside),
            device_id_type=MESH,
        )

    def part_copy(source_chip, gl, side):
        part = tbuf.at[source_chip * 2 + side, gl]
        return pltpu.make_async_remote_copy(
            src_ref=part,
            dst_ref=part,
            send_sem=part_send,
            recv_sem=part_recv.at[source_chip, gl],
            device_id=(chip * 2 + 1 - core, si),
            device_id_type=MESH,
        )

    def dual_copy(s):
        return pltpu.make_async_remote_copy(
            src_ref=dbuf.at[si],
            dst_ref=dbuf.at[si],
            send_sem=dual_send,
            recv_sem=dual_recv,
            device_id=(ti, s),
            device_id_type=MESH,
        )

    def dual_all():
        slots = dbuf.at[pl.ds(0, ns - 1)]
        return pltpu.make_async_remote_copy(
            src_ref=slots,
            dst_ref=slots,
            send_sem=dual_send,
            recv_sem=dual_recv,
            device_id=(ti, lax.rem(si + 1, ns)),
            device_id_type=MESH,
        )

    def label_copy(t):
        return pltpu.make_async_remote_copy(
            src_ref=lbuf.at[ti],
            dst_ref=lbuf.at[ti],
            send_sem=label_send,
            recv_sem=label_recv,
            device_id=(t, si),
            device_id_type=MESH,
        )

    def label_all():
        slots = lbuf.at[pl.ds(0, nt - 1)]
        return pltpu.make_async_remote_copy(
            src_ref=slots,
            dst_ref=slots,
            send_sem=label_send,
            recv_sem=label_recv,
            device_id=(chip * 2 + 1 - core, si),
            device_id_type=MESH,
        )

    def k_copy(t, s):
        return pltpu.make_async_remote_copy(
            src_ref=kbuf.at[me],
            dst_ref=kbuf.at[me],
            send_sem=k_send,
            recv_sem=k_recv,
            device_id=(t, s),
            device_id_type=MESH,
        )

    def k_all():
        others_slots = kbuf.at[pl.ds(0, ndev - 1)]
        return pltpu.make_async_remote_copy(
            src_ref=others_slots,
            dst_ref=others_slots,
            send_sem=k_send,
            recv_sem=k_recv,
            device_id=(1 - core + chip * 2, si),
            device_id_type=MESH,
        )

    band_row = lax.broadcasted_iota(jnp.int32, (LANES, LANES), 0)
    band_col = lax.broadcasted_iota(jnp.int32, (LANES, LANES), 1)
    near = (jnp.abs(band_row - band_col) <= 1) & (band_row // SIDE == band_col // SIDE)
    near = jnp.where(near, 1.0, 0.0).astype(jnp.bfloat16)
    for part in range(2):
        band[pl.ds(part * LANES, LANES), :] = near
    wide_row = lax.broadcasted_iota(jnp.int32, (LANES, per * targets), 0)
    wide_col = lax.broadcasted_iota(jnp.int32, (LANES, per * targets), 1)
    into = jnp.where(wide_col % PACK == wide_row // SIDE, 1.0, 0.0).astype(jnp.bfloat16)
    tall_row = lax.broadcasted_iota(jnp.int32, (targets, LANES), 0)
    tall_col = lax.broadcasted_iota(jnp.int32, (targets, LANES), 1)
    onto = jnp.where(tall_row % PACK == tall_col // SIDE, 1.0, 0.0).astype(jnp.bfloat16)
    for part in range(3):
        gathers[pl.ds(part * LANES, LANES), :] = into
        spread[pl.ds(part * targets, targets), :] = onto
    keep_g = lax.broadcasted_iota(jnp.int32, (groups, per * targets), 0)
    keep_t = lax.broadcasted_iota(jnp.int32, (groups, per * targets), 1)
    keep[...] = jnp.where(keep_t % targets // PACK == keep_g, 1.0, 0.0).astype(jnp.float32)
    pool = pool_hbm.shape[1] * SUB
    def choice(h):
        return lax.rem(si + h, groups_own)

    def take_group(gl):
        picks = [lax.rem(index_ref[gl * PACK + i], pool) for i in range(PACK)]
        for channel in range(CHANNELS):
            natural = [
                pool_refs[channel][at // SUB, :, pl.ds(at % SUB, 1), :].reshape(SUB, LANES)
                for at in picks
            ]
            phases = interleave(natural, mask)
            for k in range(PACK):
                tbuf[ti, gl, channel * PACK + k] = phases[k]

    loads[0].wait()
    for channel in range(CHANNELS):
        loads[4 + channel].wait()
    for h in range(0, groups_own, share):
        take_group(choice(h))

    pl.semaphore_wait(barrier, ns + chips - 1)

    def each_plane(action):
        for h in range(0, groups_own, share):
            for step in range(chips - 1, 0, -1):
                for target in (chip + step, chip - step):
                    pl.when((target >= 0) & (target < chips))(
                        functools.partial(action, choice(h), target)
                    )

    outward = (chip == 0) | (chip == chips - 2)
    edge = outward | (chip == 1) | (chip == chips - 1)
    mate = jnp.where(outward, chip + 1, chip - 1)
    direct_pairs = share == 2 and chips > 3

    def edge_copy(gl):
        part = tbuf.at[ti, gl]
        return pltpu.make_async_remote_copy(
            src_ref=part,
            dst_ref=part,
            send_sem=edge_send,
            recv_sem=plane_recv.at[chip, gl],
            device_id=(mate * 2 + core, si),
            device_id_type=MESH,
        )

    each_plane(lambda gl, target: plane_copy(chip, gl, target).start())
    for h in range(0, groups_own, share):
        part_copy(chip, choice(h), core).start()
    if share == 2:
        for h in range(1, groups_own, share):
            take_group(choice(h))
            if direct_pairs:
                pl.when(edge)(functools.partial(lambda gl: edge_copy(gl).start(), choice(h)))
            part_copy(chip, choice(h), core).start()

    loads[2].wait()

    def send_dual(step, carry):
        dual_copy(lax.rem(si + step, ns)).start()
        return carry

    lax.fori_loop(1, ns, send_dual, 0)

    loads[3].wait()
    for m in range(own_s):
        reps = []
        for channel in range(CHANNELS):
            phases = replicate(support_ref[channel, :, m, :], mask)
            reps.append(phases)
            for k in range(PACK):
                srep[channel, k, m] = phases[k] * (1.0 / (9.0 * CHANNELS))
        levels = levels_of(reps, mask)
        for layer in range(LAYERS):
            for k in range(PACK):
                inverse = lax.rsqrt(levels[layer][k])
                sroot[layer, 0, k, m] = inverse * (STRETCH / 9.0**layer)
                sroot[layer, 1, k, m] = levels[layer][k] * inverse * (9.0**layer / (STRETCH * math.pi))
                shalf[layer, k, m] = inverse * (9.0 * CHANNELS / (STRETCH * math.pi))

    def layer_map(g, layer, cross, inverse, root):
        mapped = []
        for k in range(PACK):
            x = cross[k] * (inverse[k][None] * sroot[layer, 0, k])
            size = jnp.abs(x) if layer == 0 else x
            gap = jnp.maximum(STRETCH - size, 1e-20)
            rest = STRETCH + size
            half = gap * lax.rsqrt(gap)
            poly = size + MONIC[-1]
            for term in MONIC[-2::-1]:
                poly = poly * size + term
            bend = half * poly
            slope = jnp.where(x >= 0.0, 1.0 + bend, 0.0 - bend) if layer == 0 else 1.0 + bend
            sine = half * (rest * lax.rsqrt(rest))
            scaled = sine * root[k][None]
            amp[g, layer, k] = scaled
            ang[g, layer, k] = slope
            mapped.append(scaled * sroot[layer, 1, k] + slope * cross[k])
        return mapped

    def next_cross(mapped, layer):
        return [v + BETA * 9.0**layer for v in band_sum(mapped, mask, band)]

    def finish_group(g, at, j):
        cross = [v + BETA * 9.0 for v in across([mid[j, k] for k in range(PACK)], band)]
        for layer in range(1, LAYERS):
            inverse = [tlev[at, j, layer - 1, 0, k] for k in range(PACK)]
            root = [tlev[at, j, layer - 1, 1, k] for k in range(PACK)]
            mapped = layer_map(g, layer, cross, inverse, root)
            if layer + 1 < LAYERS:
                cross = next_cross(mapped, layer + 1)
        total = (mapped[0] + mapped[1]) + (mapped[2] + mapped[3])
        ksum[:, pl.ds(g, 1), :] = jnp.sum(total, axis=1, keepdims=True)

    def begin_group(owner, gl, at, j):
        g = owner * groups_own + gl
        image = [
            [tbuf[owner, gl, channel * PACK + k] for k in range(PACK)]
            for channel in range(CHANNELS)
        ]
        levels = levels_of(image, mask)
        inverse = [[lax.rsqrt(levels[layer][k]) for k in range(PACK)] for layer in range(LAYERS)]
        root = [
            [levels[layer][k] * inverse[layer][k] for k in range(PACK)] for layer in range(LAYERS)
        ]
        for layer in range(1, LAYERS):
            for k in range(PACK):
                tlev[at, j, layer - 1, 0, k] = inverse[layer][k]
                tlev[at, j, layer - 1, 1, k] = root[layer][k]
        current = []
        for k in range(PACK):
            total = image[0][k][None] * srep[0, k]
            for channel in range(1, CHANNELS):
                total = total + image[channel][k][None] * srep[channel, k]
            current.append(total)
        cross = [v + BETA for v in band_sum(current, mask, band)]
        summed = vertical(layer_map(g, 0, cross, inverse[0], root[0]), mask)
        for k in range(PACK):
            mid[j, k] = summed[k]

    def order(n):
        both = jnp.minimum(chip, chips - 1 - chip)
        h = (n + 1) // 2
        two_sided = jnp.where(n % 2 == 1, chip - h, chip + h)
        far = n - both
        one_sided = jnp.where(chip <= chips - 1 - chip, chip + far, chip - far)
        return jnp.where(n <= 2 * both, two_sided, one_sided)

    def block(before, old, at, fresh):
        for j, g in enumerate(before):
            finish_group(g, old, j)
        for j, (owner, gl) in enumerate(fresh):
            begin_group(owner, gl, at, j)
        return tuple(owner * groups_own + gl for owner, gl in fresh)

    def near_item(n, gl, direct):
        p = order(n)
        plane_copy(p, gl, chip).wait_recv()
        if share == 2:
            apart = ((p != mate) | jnp.logical_not(edge)) if direct_pairs else True
            pl.when(direct & apart)(lambda: swap_copy(p, gl).start())
        part_copy(p, gl, core).start()
        return p * 2 + core, gl

    def far_item(n, gl):
        p = order(n)
        part_copy(p, gl, 1 - core).wait_recv()
        return p * 2 + 1 - core, gl

    slots = max(chips - 1, 1)
    before = ()
    last = slots - 1
    own = [(side, h) for side in (0, 1) for h in range(groups_own)]
    for first in range(0, len(own), 2):
        fresh = [
            far_item(0, choice(h)) if side else (ti, choice(h))
            for side, h in own[first : first + 2]
        ]
        at = (first // 2 - groups_own) % slots
        before = block(before, last, at, fresh)
        last = at

    def sweep(h, before):
        gl = choice(h)
        direct = h % 2 == 0
        items = [(side, n) for side in (0, 1) for n in range(1, chips)]
        for first in range(0, len(items), 2):
            fresh = [
                far_item(n, gl) if side else near_item(n, gl, direct)
                for side, n in items[first : first + 2]
            ]
            at = first // 2
            before = block(before, (at - 1) % slots, at, fresh)
        return before

    before = lax.fori_loop(0, groups_own, sweep, before)
    block(before, slots - 1, 0, [])

    nt_dims = (((1,), (1,)), ((), ()))
    lane_sums = jnp.dot(
        split_rows(ksum[...].reshape(own_s * groups, LANES)), gathers[...],
        preferred_element_type=jnp.float32,
    ) * (1.0 / (PIXELS * 9.0 ** (LAYERS - 1)))
    picked = jnp.sum(lane_sums.reshape(own_s, groups, per * targets) * keep[...][None], axis=1)
    half = lax.broadcasted_iota(jnp.int32, (1, per * targets), 1) // targets
    for r in range(own_s // per):
        packed = picked[r * per : r * per + 1]
        for h in range(1, per):
            packed = jnp.where(half == h, picked[r * per + h : r * per + h + 1], packed)
        kbuf[me, pl.ds(r, 1), :] = packed

    for dt in sorted(range(nt), key=lambda d: -min(d, nt - d)):
        for ds in range(ns - 1, -1, -1):
            if dt or ds:
                k_copy(lax.rem(ti + dt, nt), lax.rem(si + ds, ns)).start()

    loads[1].wait()
    row = lax.broadcasted_iota(jnp.int32, (SUB, LANES), 0)
    lane = lax.broadcasted_iota(jnp.int32, (SUB, LANES), 1)
    line = lax.broadcasted_iota(jnp.int32, (1, LANES), 1)
    label = jnp.zeros((SUB, LANES), jnp.int32)
    labels = jnp.zeros((1, LANES), jnp.int32)
    for r in range(own_t):
        value = label_ref[r]
        label = jnp.where(row == r, value, label)
        labels = jnp.where(line == ti * own_t + r, value, labels)
    own_onehot = jnp.where(label == lane, 1.0, 0.0).astype(jnp.float32)
    lbuf[ti] = labels

    def send_label(step, carry):
        label_copy(lax.rem(ti + step, nt)).start()
        return carry

    lax.fori_loop(1, nt, send_label, 0)

    def pair_step(step, stages):
        ready = [at - 1 for at in stages if at > 0]
        levels, passes = [
            dict(zip(
                [(at, k) for at in ready for k in range(PACK)],
                across([held[which, at, k] for at in ready for k in range(PACK)], band)
                if ready else [],
            ))
            for which in range(2)
        ]
        for at in sorted(stages, reverse=True):
            g = step - at
            if at == LAYERS:
                owner = g // groups_own
                gl = g % groups_own
                for channel in range(CHANNELS):
                    for k in range(PACK):
                        image = tbuf[owner, gl, channel * PACK + k]
                        unit[g, channel, k] = (
                            passes[at - 1, k] * image[None] + srep[channel, k] * levels[at - 1, k]
                        )
                continue
            layer = LAYERS - 1 - at
            term = [amp[g, layer, k] * shalf[layer, k] for k in range(PACK)]
            slope = [ang[g, layer, k] for k in range(PACK)]
            if at > 0:
                term = [t * passes[at - 1, k] + levels[at - 1, k] for k, t in enumerate(term)]
                slope = [v * passes[at - 1, k] for k, v in enumerate(slope)]
            for k, v in enumerate(vertical(term, mask)):
                held[0, at, k] = v
            for k, v in enumerate(vertical(slope, mask)):
                held[1, at, k] = v

    span = 2
    whole = max(groups - LAYERS, 0) // span

    def pair_unit(trip, carry):
        for extra in range(span):
            pair_step(LAYERS + trip * span + extra, range(LAYERS + 1))
        return carry

    for step in range(min(LAYERS, groups)):
        pair_step(step, range(step + 1))
    lax.fori_loop(0, whole, pair_unit, 0)
    for step in range(LAYERS + whole * span, groups):
        pair_step(step, range(LAYERS + 1))
    for step in range(groups, groups + LAYERS):
        pair_step(step, range(step - groups + 1, LAYERS + 1))

    dual_all().wait_recv()
    rows = dual_hbm.shape[0] // per

    def dual_rows(h):
        if per == 1:
            return dbuf[...].reshape(ns * rows, CLASSES)
        return jnp.concatenate([dbuf[s, pl.ds(h, rows, stride=per), :] for s in range(ns)], axis=0)

    own_duals = dbuf[si, pl.ds(ti * own_s, own_s), :]
    gram = jnp.concatenate(
        [
            lax.dot_general(
                own_duals, dual_rows(h), nt_dims, precision=HIGH, preferred_element_type=jnp.float32
            )
            for h in range(per)
        ],
        axis=0,
    )
    top, middle, bottom = split_parts(gram)
    blank = jnp.zeros_like(top)
    factors = jnp.concatenate(
        [
            jnp.concatenate([top, top, top], axis=1),
            jnp.concatenate([middle, middle, blank], axis=1),
            jnp.concatenate([bottom, blank, blank], axis=1),
        ],
        axis=0,
    )
    label_all().wait_recv()
    named = lbuf[0]
    for t in range(1, nt):
        named = named + lbuf[t]
    classes = lax.broadcasted_iota(jnp.int32, (CLASSES, targets), 0)
    onehot = jnp.where(classes == named[:, :targets], 1.0, 0.0).astype(jnp.float32)
    offset = jnp.dot(own_duals, onehot, precision=HIGH, preferred_element_type=jnp.float32)

    def sent(sem, count, width):
        part = tbuf.at[pl.ds(0, count), pl.ds(0, width)]
        pltpu.make_async_remote_copy(
            src_ref=part,
            dst_ref=part,
            send_sem=sem,
            recv_sem=plane_recv.at[chip, 0],
            device_id=(chip * 2 + 1 - core, si),
            device_id_type=MESH,
        ).wait_send()

    sent(plane_send, chips - 1, groups_own // share)
    if share == 2:
        half = groups_own // share
        if direct_pairs:
            pl.when(edge)(lambda: sent(swap_send, chips - 2, half))
            pl.when(edge)(lambda: sent(edge_send, 1, half))
            pl.when(jnp.logical_not(edge))(lambda: sent(swap_send, chips - 1, half))
        else:
            sent(swap_send, chips - 1, half)
    sent(part_send, chips, groups_own)
    dual_all().wait_send()
    label_all().wait_send()
    k_all().wait_send()

    k_all().wait_recv()
    columns = jnp.concatenate([kbuf[d] for d in range(ndev)], axis=0)
    three = jnp.dot(
        factors, jnp.concatenate(split_parts(columns), axis=0), preferred_element_type=jnp.float32
    )
    span = per * own_s
    both = (three[2 * span :] + three[span : 2 * span]) + three[:span]
    weight = -offset
    for h in range(per):
        weight = weight + both[h * own_s : (h + 1) * own_s, h * targets : (h + 1) * targets]
    weight = weight * (1.0 / (CHANNELS * 9.0**LAYERS))
    wide = (weight[:, None, :] * keep[:, :targets][None]).reshape(own_s * groups, targets)
    wexp[...] = jnp.dot(split_rows(wide), spread[...], preferred_element_type=jnp.float32)
    pred[...] = columns.T

    even = mask[4] % 2 == 0
    early = mask[4] < 2
    for m in range(own_s):
        sums = [[None] * PACK for _ in range(CHANNELS)]
        for g in range(groups):
            w = wexp[pl.ds(m * groups + g, SUB, stride=0), :]
            for channel in range(CHANNELS):
                for k in range(PACK):
                    value = w * unit[g, channel, k, m]
                    sums[channel][k] = value if g == 0 else sums[channel][k] + value
        for channel in range(CHANNELS):
            low = fold(sums[channel][0], sums[channel][1], even, SIDE)
            high = fold(sums[channel][2], sums[channel][3], even, SIDE)
            flat[channel, m] = fold(low, high, early, 2 * SIDE)
    residual = -own_onehot[:own_t, :CLASSES]
    for h in range(per):
        residual = residual + jnp.dot(
            pred[pl.ds(h * targets + ti * own_t, own_t), :], dual_rows(h),
            precision=HIGH, preferred_element_type=jnp.float32,
        )
    residual_ref[...] = residual
    for channel in range(CHANNELS):
        for s in range(SUB):
            grad_ref[channel, s] = flat[channel, :, s, :]


def hand_over(residual_ref, grad_ref, residual_out, grad_out):
    residual_out[...] = residual_ref[...]
    grad_out[...] = grad_ref[...]


def shards(nt, ns, target_pool, target_index, target_labels, dual_weights, support_images):
    own_t = target_index.shape[0]
    own_s = support_images.shape[0]
    groups_own = own_t // PACK
    groups = nt * groups_own
    chips = nt // 2
    ndev = nt * ns
    per = sharing(nt * own_t, own_s)
    f32 = jnp.float32
    vmem = pl.BlockSpec(memory_space=pltpu.VMEM)
    hbm = pl.BlockSpec(memory_space=pltpu.HBM)
    dma = pltpu.SemaphoreType.DMA
    tile = (SUB, LANES)
    pool = target_pool.reshape(-1, SUB, CHANNELS, SUB, LANES).transpose(2, 0, 3, 1, 4)
    support = support_images.reshape(own_s, CHANNELS, SUB, LANES).transpose(1, 2, 0, 3)
    residual, grad = pl.pallas_call(
        functools.partial(kernel, nt, ns, own_t, own_s),
        out_shape=(
            jax.ShapeDtypeStruct((own_t, CLASSES), f32),
            jax.ShapeDtypeStruct((CHANNELS, SUB, own_s, LANES), f32),
        ),
        in_specs=[hbm] * 5,
        out_specs=(vmem, vmem),
        scratch_shapes=[
            pltpu.SMEM((own_t,), jnp.int32),
            pltpu.SMEM((own_t,), jnp.int32),
            *[pltpu.VMEM(pool.shape[1:], f32)] * CHANNELS,
            pltpu.VMEM(support.shape, f32),
            pltpu.VMEM((nt, groups_own, CHANNELS * PACK) + tile, f32),
            pltpu.VMEM((ns,) + dual_weights.shape, f32),
            pltpu.VMEM((nt, 1, LANES), jnp.int32),
            pltpu.VMEM((ndev, own_s // per, per * nt * own_t), f32),
            pltpu.VMEM((2 * LANES, LANES), jnp.bfloat16),
            pltpu.VMEM((3 * LANES, per * nt * own_t), jnp.bfloat16),
            pltpu.VMEM((3 * nt * own_t, LANES), jnp.bfloat16),
            pltpu.VMEM((groups, per * nt * own_t), f32),
            pltpu.VMEM((CHANNELS, PACK, own_s) + tile, f32),
            pltpu.VMEM((LAYERS, 2, PACK, own_s) + tile, f32),
            pltpu.VMEM((LAYERS, PACK, own_s) + tile, f32),
            pltpu.VMEM((max(chips - 1, 1), 2, LAYERS - 1, 2, PACK) + tile, f32),
            pltpu.VMEM((2, PACK, own_s) + tile, f32),
            pltpu.VMEM((2, LAYERS, PACK, own_s) + tile, f32),
            pltpu.VMEM((groups, LAYERS, PACK, own_s) + tile, f32),
            pltpu.VMEM((groups, LAYERS, PACK, own_s) + tile, f32),
            pltpu.VMEM((groups, CHANNELS, PACK, own_s) + tile, f32),
            pltpu.VMEM((own_s, groups, LANES), f32),
            pltpu.VMEM((own_s * groups, LANES), f32),
            pltpu.VMEM((per * nt * own_t, ns * dual_weights.shape[0] // per), f32),
            pltpu.VMEM((CHANNELS, own_s) + tile, f32),
            dma((4 + CHANNELS,)),
            dma,
            dma((chips, groups_own)),
            dma,
            dma,
            dma,
            dma((chips, groups_own)),
            dma,
            dma,
            dma,
            dma,
            dma,
            dma,
        ],
        compiler_params=pltpu.CompilerParams(
            collective_id=0, has_side_effects=True, vmem_limit_bytes=44 * 2**20
        ),
    )(*[
        pltpu.with_memory_space_constraint(v, pltpu.HBM)
        for v in (target_index, target_labels, pool, dual_weights, support)
    ])
    residual, grad = pl.pallas_call(
        hand_over,
        out_shape=(
            jax.ShapeDtypeStruct(residual.shape, f32),
            jax.ShapeDtypeStruct(grad.shape, f32),
        ),
        in_specs=[vmem, vmem],
        out_specs=(vmem, vmem),
        compiler_params=pltpu.CompilerParams(vmem_limit_bytes=2**20),
    )(residual, grad)
    return (residual, grad.transpose(2, 0, 1, 3).reshape(support_images.shape))


def solution(mesh):
    in_specs = (
        P("tgt", None, None),
        P("tgt"),
        P("tgt"),
        P("sup", None),
        P(("sup", "tgt"), None, None),
    )
    out_specs = (P("tgt", None), P(("sup", "tgt"), None, None))
    body = functools.partial(shards, mesh.shape["tgt"], mesh.shape["sup"])
    return jax.shard_map(body, mesh=mesh, in_specs=in_specs, out_specs=out_specs, check_vma=False)
```

```python
import functools
import math

import jax
import jax.numpy as jnp
from jax import lax
from jax.experimental import pallas as pl
from jax.experimental.pallas import tpu as pltpu
from jax.sharding import PartitionSpec as P

CHANNELS = 3
SIDE = 32
CLASSES = 100
LAYERS = 3
PIXELS = 1024
BETA = 0.01
PACK = 4
SUB = 8
LANES = 128
MESH = pl.DeviceIdType.MESH
HIGH = lax.Precision.HIGHEST
ACOS = (
    1.5707956895,
    -0.2145428158,
    0.0881710453,
    -0.0459272047,
    0.0206200335,
    -0.0049111629,
)


STRETCH = (-ACOS[-1] / math.pi) ** (2.0 / (2 * len(ACOS) - 1))
MONIC = [
    term / ACOS[-1] * STRETCH ** (len(ACOS) - 1 - power) for power, term in enumerate(ACOS)
][:-1]


def masks():
    lane = lax.broadcasted_iota(jnp.int32, (SUB, LANES), 1)
    row = lax.broadcasted_iota(jnp.int32, (SUB, LANES), 0)
    column = lane % SIDE
    return (column > 0, column < SIDE - 1, row > 0, row < SUB - 1, lane // SIDE)


def box_sum(maps, mask):
    right, left, down, up, _ = mask
    axis = maps[0].ndim - 1

    def across(v):
        return (
            v
            + jnp.where(right, pltpu.roll(v, 1, axis), 0.0)
            + jnp.where(left, pltpu.roll(v, LANES - 1, axis), 0.0)
        )

    before = jnp.where(down, pltpu.roll(maps[3], 1, axis - 1), 0.0)
    after = jnp.where(up, pltpu.roll(maps[0], SUB - 1, axis - 1), 0.0)
    low = maps[0] + maps[1]
    high = maps[2] + maps[3]
    return [across(v) for v in (before + low, low + maps[2], maps[1] + high, high + after)]


def vertical(maps, mask):
    down, up = mask[2], mask[3]
    axis = maps[0].ndim - 2
    before = jnp.where(down, pltpu.roll(maps[3], 1, axis), 0.0)
    after = jnp.where(up, pltpu.roll(maps[0], SUB - 1, axis), 0.0)
    low = maps[0] + maps[1]
    high = maps[2] + maps[3]
    return [before + low, low + maps[2], maps[1] + high, high + after]


def band_sum(maps, mask, band):
    return across(vertical(maps, mask), band)


def across(maps, band):
    shape = maps[0].shape
    rows = jnp.stack(maps).reshape(-1, LANES)
    high = rows.astype(jnp.bfloat16)
    low = (rows - high.astype(jnp.float32)).astype(jnp.bfloat16)
    out = jnp.dot(
        jnp.concatenate([high, low], axis=1), band[...], preferred_element_type=jnp.float32
    ).reshape((len(maps),) + shape)
    return [out[k] for k in range(len(maps))]


def interleave(images, mask):
    group = mask[4]
    out = []
    for k in range(PACK):
        total = None
        for m in range(PACK):
            shift = ((m - k) * SIDE) % LANES
            moved = images[m] if shift == 0 else pltpu.roll(images[m], shift, 1)
            total = moved if total is None else jnp.where(group == m, moved, total)
        out.append(total)
    return out


def replicate(image, mask):
    group = mask[4]
    out = []
    rolled = [image] + [pltpu.roll(image, SIDE * s, 1) for s in range(1, PACK)]
    for k in range(PACK):
        total = None
        for m in range(PACK):
            moved = rolled[(m - k) % PACK]
            total = moved if total is None else jnp.where(group == m, moved, total)
        out.append(total)
    return out


def levels_of(images, mask):
    energy = []
    for k in range(PACK):
        total = images[0][k] * images[0][k]
        for channel in range(1, CHANNELS):
            total = total + images[channel][k] * images[channel][k]
        energy.append(total * (1.0 / CHANNELS))
    levels = []
    current = energy
    for _ in range(LAYERS):
        current = [v * (1.0 / 9.0) + BETA for v in box_sum(current, mask)]
        levels.append(current)
    return levels


def sharing(targets, own_s):
    per = max(LANES // targets, 1)
    return per if LANES % targets == 0 and own_s % per == 0 else 1


def split_parts(v):
    high = v.astype(jnp.bfloat16)
    rest = v - high.astype(jnp.float32)
    middle = rest.astype(jnp.bfloat16)
    return high, middle, (rest - middle.astype(jnp.float32)).astype(jnp.bfloat16)


def split_rows(v):
    return jnp.concatenate(split_parts(v), axis=1)


def fold(a, b, keep, shift):
    return jnp.where(keep, a, b) + pltpu.roll(jnp.where(keep, b, a), shift, a.ndim - 1)


def kernel(
    nt, ns, own_t, own_s,
    index_hbm, label_hbm, pool_hbm, dual_hbm, support_hbm,
    residual_ref, grad_ref,
    index_ref, label_ref, pool_a, pool_b, pool_c, support_ref,
    tbuf, dbuf, lbuf, kbuf, band, gathers, spread, keep, srep, sroot, shalf, tlev, mid, held, amp, ang, unit, ksum, wexp, pred, flat,
    in_sem, plane_send, plane_recv, swap_send, edge_send, part_send, part_recv,
    dual_send, dual_recv, label_send, label_recv, k_send, k_recv,
):
    ti = lax.axis_index("tgt")
    si = lax.axis_index("sup")
    pool_refs = (pool_a, pool_b, pool_c)
    chips = nt // 2
    chip = ti // 2
    core = ti % 2
    ndev = nt * ns
    me = si * nt + ti
    groups_own = own_t // PACK
    groups = nt * groups_own
    targets = nt * own_t
    per = sharing(targets, own_s)
    mask = masks()
    share = 2 if groups_own % 2 == 0 and ns % 2 == 0 else 1
    beside = si + 1 - 2 * (si % 2)
    barrier = pltpu.get_barrier_semaphore()

    def greet(t, s):
        pl.semaphore_signal(barrier, inc=1, device_id=(t, s), device_id_type=MESH)

    def fetch(at, src, dst):
        return pltpu.make_async_copy(src, dst, in_sem.at[at])

    loads = [
        fetch(0, index_hbm, index_ref),
        fetch(1, label_hbm, label_ref),
        fetch(2, dual_hbm, dbuf.at[si]),
        fetch(3, support_hbm, support_ref),
    ] + [fetch(4 + c, pool_hbm.at[c], pool_refs[c]) for c in range(CHANNELS)]
    for at in (0, 4, 5, 6):
        loads[at].start()

    for step in range(1, ns):
        greet(ti, lax.rem(si + step, ns))
    greet(chip * 2 + 1 - core, si)
    for step in range(1, chips):
        greet(lax.rem(ti + 2 * step, nt), si)

    for at in (3, 2, 1):
        loads[at].start()

    def plane_copy(source_chip, gl, target_chip):
        part = tbuf.at[source_chip * 2 + core, gl]
        return pltpu.make_async_remote_copy(
            src_ref=part,
            dst_ref=part,
            send_sem=plane_send,
            recv_sem=plane_recv.at[source_chip, gl],
            device_id=(target_chip * 2 + core, si),
            device_id_type=MESH,
        )

    def swap_copy(source_chip, gl):
        part = tbuf.at[source_chip * 2 + core, gl]
        return pltpu.make_async_remote_copy(
            src_ref=part,
            dst_ref=part,
            send_sem=swap_send,
            recv_sem=plane_recv.at[source_chip, gl],
            device_id=(ti, beside),
            device_id_type=MESH,
        )

    def part_copy(source_chip, gl, side):
        part = tbuf.at[source_chip * 2 + side, gl]
        return pltpu.make_async_remote_copy(
            src_ref=part,
            dst_ref=part,
            send_sem=part_send,
            recv_sem=part_recv.at[source_chip, gl],
            device_id=(chip * 2 + 1 - core, si),
            device_id_type=MESH,
        )

    def dual_copy(s):
        return pltpu.make_async_remote_copy(
            src_ref=dbuf.at[si],
            dst_ref=dbuf.at[si],
            send_sem=dual_send,
            recv_sem=dual_recv,
            device_id=(ti, s),
            device_id_type=MESH,
        )

    def dual_all():
        slots = dbuf.at[pl.ds(0, ns - 1)]
        return pltpu.make_async_remote_copy(
            src_ref=slots,
            dst_ref=slots,
            send_sem=dual_send,
            recv_sem=dual_recv,
            device_id=(ti, lax.rem(si + 1, ns)),
            device_id_type=MESH,
        )

    def label_copy(t):
        return pltpu.make_async_remote_copy(
            src_ref=lbuf.at[ti],
            dst_ref=lbuf.at[ti],
            send_sem=label_send,
            recv_sem=label_recv,
            device_id=(t, si),
            device_id_type=MESH,
        )

    def label_all():
        slots = lbuf.at[pl.ds(0, nt - 1)]
        return pltpu.make_async_remote_copy(
            src_ref=slots,
            dst_ref=slots,
            send_sem=label_send,
            recv_sem=label_recv,
            device_id=(chip * 2 + 1 - core, si),
            device_id_type=MESH,
        )

    def k_copy(t, s):
        return pltpu.make_async_remote_copy(
            src_ref=kbuf.at[me],
            dst_ref=kbuf.at[me],
            send_sem=k_send,
            recv_sem=k_recv,
            device_id=(t, s),
            device_id_type=MESH,
        )

    def k_all():
        others_slots = kbuf.at[pl.ds(0, ndev - 1)]
        return pltpu.make_async_remote_copy(
            src_ref=others_slots,
            dst_ref=others_slots,
            send_sem=k_send,
            recv_sem=k_recv,
            device_id=(1 - core + chip * 2, si),
            device_id_type=MESH,
        )

    band_row = lax.broadcasted_iota(jnp.int32, (LANES, LANES), 0)
    band_col = lax.broadcasted_iota(jnp.int32, (LANES, LANES), 1)
    near = (jnp.abs(band_row - band_col) <= 1) & (band_row // SIDE == band_col // SIDE)
    near = jnp.where(near, 1.0, 0.0).astype(jnp.bfloat16)
    for part in range(2):
        band[pl.ds(part * LANES, LANES), :] = near
    wide_row = lax.broadcasted_iota(jnp.int32, (LANES, per * targets), 0)
    wide_col = lax.broadcasted_iota(jnp.int32, (LANES, per * targets), 1)
    into = jnp.where(wide_col % PACK == wide_row // SIDE, 1.0, 0.0).astype(jnp.bfloat16)
    tall_row = lax.broadcasted_iota(jnp.int32, (targets, LANES), 0)
    tall_col = lax.broadcasted_iota(jnp.int32, (targets, LANES), 1)
    onto = jnp.where(tall_row % PACK == tall_col // SIDE, 1.0, 0.0).astype(jnp.bfloat16)
    for part in range(3):
        gathers[pl.ds(part * LANES, LANES), :] = into
        spread[pl.ds(part * targets, targets), :] = onto
    keep_g = lax.broadcasted_iota(jnp.int32, (groups, per * targets), 0)
    keep_t = lax.broadcasted_iota(jnp.int32, (groups, per * targets), 1)
    keep[...] = jnp.where(keep_t % targets // PACK == keep_g, 1.0, 0.0).astype(jnp.float32)
    pool = pool_hbm.shape[1] * SUB
    def choice(h):
        return lax.rem(si + h, groups_own)

    def take_group(gl):
        picks = [lax.rem(index_ref[gl * PACK + i], pool) for i in range(PACK)]
        for channel in range(CHANNELS):
            natural = [
                pool_refs[channel][at // SUB, :, pl.ds(at % SUB, 1), :].reshape(SUB, LANES)
                for at in picks
            ]
            phases = interleave(natural, mask)
            for k in range(PACK):
                tbuf[ti, gl, channel * PACK + k] = phases[k]

    loads[0].wait()
    for channel in range(CHANNELS):
        loads[4 + channel].wait()
    for h in range(0, groups_own, share):
        take_group(choice(h))

    pl.semaphore_wait(barrier, ns + chips - 1)

    def each_plane(action):
        for h in range(0, groups_own, share):
            for step in range(chips - 1, 0, -1):
                for target in (chip + step, chip - step):
                    pl.when((target >= 0) & (target < chips))(
                        functools.partial(action, choice(h), target)
                    )

    outward = (chip == 0) | (chip == chips - 2)
    edge = outward | (chip == 1) | (chip == chips - 1)
    mate = jnp.where(outward, chip + 1, chip - 1)
    direct_pairs = share == 2 and chips > 3

    def edge_copy(gl):
        part = tbuf.at[ti, gl]
        return pltpu.make_async_remote_copy(
            src_ref=part,
            dst_ref=part,
            send_sem=edge_send,
            recv_sem=plane_recv.at[chip, gl],
            device_id=(mate * 2 + core, si),
            device_id_type=MESH,
        )

    each_plane(lambda gl, target: plane_copy(chip, gl, target).start())
    for h in range(0, groups_own, share):
        part_copy(chip, choice(h), core).start()
    if share == 2:
        for h in range(1, groups_own, share):
            take_group(choice(h))
            if direct_pairs:
                pl.when(edge)(functools.partial(lambda gl: edge_copy(gl).start(), choice(h)))
            part_copy(chip, choice(h), core).start()

    loads[2].wait()

    def send_dual(step, carry):
        dual_copy(lax.rem(si + step, ns)).start()
        return carry

    lax.fori_loop(1, ns, send_dual, 0)

    loads[3].wait()
    for m in range(own_s):
        reps = []
        for channel in range(CHANNELS):
            phases = replicate(support_ref[channel, :, m, :], mask)
            reps.append(phases)
            for k in range(PACK):
                srep[channel, k, m] = phases[k] * (1.0 / (9.0 * CHANNELS))
        levels = levels_of(reps, mask)
        for layer in range(LAYERS):
            for k in range(PACK):
                inverse = lax.rsqrt(levels[layer][k])
                sroot[layer, 0, k, m] = inverse * (STRETCH / 9.0**layer)
                sroot[layer, 1, k, m] = levels[layer][k] * inverse * (9.0**layer / (STRETCH * math.pi))
                shalf[layer, k, m] = inverse * (9.0 * CHANNELS / (STRETCH * math.pi))

    def layer_map(g, layer, cross, inverse, root):
        mapped = []
        for k in range(PACK):
            x = cross[k] * (inverse[k][None] * sroot[layer, 0, k])
            size = jnp.abs(x) if layer == 0 else x
            gap = jnp.maximum(STRETCH - size, 1e-20)
            rest = STRETCH + size
            half = gap * lax.rsqrt(gap)
            poly = size + MONIC[-1]
            for term in MONIC[-2::-1]:
                poly = poly * size + term
            bend = half * poly
            slope = jnp.where(x >= 0.0, 1.0 + bend, 0.0 - bend) if layer == 0 else 1.0 + bend
            sine = half * (rest * lax.rsqrt(rest))
            scaled = sine * root[k][None]
            amp[g, layer, k] = scaled
            ang[g, layer, k] = slope
            mapped.append(scaled * sroot[layer, 1, k] + slope * cross[k])
        return mapped

    def next_cross(mapped, layer):
        return [v + BETA * 9.0**layer for v in band_sum(mapped, mask, band)]

    def finish_group(g, at, j):
        cross = [v + BETA * 9.0 for v in across([mid[j, k] for k in range(PACK)], band)]
        for layer in range(1, LAYERS):
            inverse = [tlev[at, j, layer - 1, 0, k] for k in range(PACK)]
            root = [tlev[at, j, layer - 1, 1, k] for k in range(PACK)]
            mapped = layer_map(g, layer, cross, inverse, root)
            if layer + 1 < LAYERS:
                cross = next_cross(mapped, layer + 1)
        total = (mapped[0] + mapped[1]) + (mapped[2] + mapped[3])
        ksum[:, pl.ds(g, 1), :] = jnp.sum(total, axis=1, keepdims=True)

    def begin_group(owner, gl, at, j):
        g = owner * groups_own + gl
        image = [
            [tbuf[owner, gl, channel * PACK + k] for k in range(PACK)]
            for channel in range(CHANNELS)
        ]
        levels = levels_of(image, mask)
        inverse = [[lax.rsqrt(levels[layer][k]) for k in range(PACK)] for layer in range(LAYERS)]
        root = [
            [levels[layer][k] * inverse[layer][k] for k in range(PACK)] for layer in range(LAYERS)
        ]
        for layer in range(1, LAYERS):
            for k in range(PACK):
                tlev[at, j, layer - 1, 0, k] = inverse[layer][k]
                tlev[at, j, layer - 1, 1, k] = root[layer][k]
        current = []
        for k in range(PACK):
            total = image[0][k][None] * srep[0, k]
            for channel in range(1, CHANNELS):
                total = total + image[channel][k][None] * srep[channel, k]
            current.append(total)
        cross = [v + BETA for v in band_sum(current, mask, band)]
        summed = vertical(layer_map(g, 0, cross, inverse[0], root[0]), mask)
        for k in range(PACK):
            mid[j, k] = summed[k]

    def order(n):
        both = jnp.minimum(chip, chips - 1 - chip)
        h = (n + 1) // 2
        two_sided = jnp.where(n % 2 == 1, chip - h, chip + h)
        far = n - both
        one_sided = jnp.where(chip <= chips - 1 - chip, chip + far, chip - far)
        return jnp.where(n <= 2 * both, two_sided, one_sided)

    def block(before, old, at, fresh):
        for j, g in enumerate(before):
            finish_group(g, old, j)
        for j, (owner, gl) in enumerate(fresh):
            begin_group(owner, gl, at, j)
        return tuple(owner * groups_own + gl for owner, gl in fresh)

    def near_item(n, gl, direct):
        p = order(n)
        plane_copy(p, gl, chip).wait_recv()
        if share == 2:
            apart = ((p != mate) | jnp.logical_not(edge)) if direct_pairs else True
            pl.when(direct & apart)(lambda: swap_copy(p, gl).start())
        part_copy(p, gl, core).start()
        return p * 2 + core, gl

    def far_item(n, gl):
        p = order(n)
        part_copy(p, gl, 1 - core).wait_recv()
        return p * 2 + 1 - core, gl

    slots = max(chips - 1, 1)
    before = ()
    last = slots - 1
    own = [(side, h) for side in (0, 1) for h in range(groups_own)]
    for first in range(0, len(own), 2):
        fresh = [
            far_item(0, choice(h)) if side else (ti, choice(h))
            for side, h in own[first : first + 2]
        ]
        at = (first // 2 - groups_own) % slots
        before = block(before, last, at, fresh)
        last = at

    def sweep(h, before):
        gl = choice(h)
        direct = h % 2 == 0
        items = [(side, n) for side in (0, 1) for n in range(1, chips)]
        for first in range(0, len(items), 2):
            fresh = [
                far_item(n, gl) if side else near_item(n, gl, direct)
                for side, n in items[first : first + 2]
            ]
            at = first // 2
            before = block(before, (at - 1) % slots, at, fresh)
        return before

    before = lax.fori_loop(0, groups_own, sweep, before)
    block(before, slots - 1, 0, [])

    nt_dims = (((1,), (1,)), ((), ()))
    lane_sums = jnp.dot(
        split_rows(ksum[...].reshape(own_s * groups, LANES)), gathers[...],
        preferred_element_type=jnp.float32,
    ) * (1.0 / (PIXELS * 9.0 ** (LAYERS - 1)))
    picked = jnp.sum(lane_sums.reshape(own_s, groups, per * targets) * keep[...][None], axis=1)
    half = lax.broadcasted_iota(jnp.int32, (1, per * targets), 1) // targets
    for r in range(own_s // per):
        packed = picked[r * per : r * per + 1]
        for h in range(1, per):
            packed = jnp.where(half == h, picked[r * per + h : r * per + h + 1], packed)
        kbuf[me, pl.ds(r, 1), :] = packed

    for dt in sorted(range(nt), key=lambda d: -min(d, nt - d)):
        for ds in range(ns - 1, -1, -1):
            if dt or ds:
                k_copy(lax.rem(ti + dt, nt), lax.rem(si + ds, ns)).start()

    loads[1].wait()
    row = lax.broadcasted_iota(jnp.int32, (SUB, LANES), 0)
    lane = lax.broadcasted_iota(jnp.int32, (SUB, LANES), 1)
    line = lax.broadcasted_iota(jnp.int32, (1, LANES), 1)
    label = jnp.zeros((SUB, LANES), jnp.int32)
    labels = jnp.zeros((1, LANES), jnp.int32)
    for r in range(own_t):
        value = label_ref[r]
        label = jnp.where(row == r, value, label)
        labels = jnp.where(line == ti * own_t + r, value, labels)
    own_onehot = jnp.where(label == lane, 1.0, 0.0).astype(jnp.float32)
    lbuf[ti] = labels

    def send_label(step, carry):
        label_copy(lax.rem(ti + step, nt)).start()
        return carry

    lax.fori_loop(1, nt, send_label, 0)

    def pair_step(step, stages):
        ready = [at - 1 for at in stages if at > 0]
        levels, passes = [
            dict(zip(
                [(at, k) for at in ready for k in range(PACK)],
                across([held[which, at, k] for at in ready for k in range(PACK)], band)
                if ready else [],
            ))
            for which in range(2)
        ]
        for at in sorted(stages, reverse=True):
            g = step - at
            if at == LAYERS:
                owner = g // groups_own
                gl = g % groups_own
                for channel in range(CHANNELS):
                    for k in range(PACK):
                        image = tbuf[owner, gl, channel * PACK + k]
                        unit[g, channel, k] = (
                            passes[at - 1, k] * image[None] + srep[channel, k] * levels[at - 1, k]
                        )
                continue
            layer = LAYERS - 1 - at
            term = [amp[g, layer, k] * shalf[layer, k] for k in range(PACK)]
            slope = [ang[g, layer, k] for k in range(PACK)]
            if at > 0:
                term = [t * passes[at - 1, k] + levels[at - 1, k] for k, t in enumerate(term)]
                slope = [v * passes[at - 1, k] for k, v in enumerate(slope)]
            for k, v in enumerate(vertical(term, mask)):
                held[0, at, k] = v
            for k, v in enumerate(vertical(slope, mask)):
                held[1, at, k] = v

    span = 4
    whole = max(groups - LAYERS, 0) // span

    def pair_unit(trip, carry):
        for extra in range(span):
            pair_step(LAYERS + trip * span + extra, range(LAYERS + 1))
        return carry

    for step in range(min(LAYERS, groups)):
        pair_step(step, range(step + 1))
    lax.fori_loop(0, whole, pair_unit, 0)
    for step in range(LAYERS + whole * span, groups):
        pair_step(step, range(LAYERS + 1))
    for step in range(groups, groups + LAYERS):
        pair_step(step, range(step - groups + 1, LAYERS + 1))

    dual_all().wait_recv()
    rows = dual_hbm.shape[0] // per

    def dual_rows(h):
        if per == 1:
            return dbuf[...].reshape(ns * rows, CLASSES)
        return jnp.concatenate([dbuf[s, pl.ds(h, rows, stride=per), :] for s in range(ns)], axis=0)

    own_duals = dbuf[si, pl.ds(ti * own_s, own_s), :]
    gram = jnp.concatenate(
        [
            lax.dot_general(
                own_duals, dual_rows(h), nt_dims, precision=HIGH, preferred_element_type=jnp.float32
            )
            for h in range(per)
        ],
        axis=0,
    )
    top, middle, bottom = split_parts(gram)
    blank = jnp.zeros_like(top)
    factors = jnp.concatenate(
        [
            jnp.concatenate([top, top, top], axis=1),
            jnp.concatenate([middle, middle, blank], axis=1),
            jnp.concatenate([bottom, blank, blank], axis=1),
        ],
        axis=0,
    )
    label_all().wait_recv()
    named = lbuf[0]
    for t in range(1, nt):
        named = named + lbuf[t]
    classes = lax.broadcasted_iota(jnp.int32, (CLASSES, targets), 0)
    onehot = jnp.where(classes == named[:, :targets], 1.0, 0.0).astype(jnp.float32)
    offset = jnp.dot(own_duals, onehot, precision=HIGH, preferred_element_type=jnp.float32)

    def sent(sem, count, width):
        part = tbuf.at[pl.ds(0, count), pl.ds(0, width)]
        pltpu.make_async_remote_copy(
            src_ref=part,
            dst_ref=part,
            send_sem=sem,
            recv_sem=plane_recv.at[chip, 0],
            device_id=(chip * 2 + 1 - core, si),
            device_id_type=MESH,
        ).wait_send()

    sent(plane_send, chips - 1, groups_own // share)
    if share == 2:
        half = groups_own // share
        if direct_pairs:
            pl.when(edge)(lambda: sent(swap_send, chips - 2, half))
            pl.when(edge)(lambda: sent(edge_send, 1, half))
            pl.when(jnp.logical_not(edge))(lambda: sent(swap_send, chips - 1, half))
        else:
            sent(swap_send, chips - 1, half)
    sent(part_send, chips, groups_own)
    dual_all().wait_send()
    label_all().wait_send()
    k_all().wait_send()

    k_all().wait_recv()
    columns = jnp.concatenate([kbuf[d] for d in range(ndev)], axis=0)
    three = jnp.dot(
        factors, jnp.concatenate(split_parts(columns), axis=0), preferred_element_type=jnp.float32
    )
    span = per * own_s
    both = (three[2 * span :] + three[span : 2 * span]) + three[:span]
    weight = -offset
    for h in range(per):
        weight = weight + both[h * own_s : (h + 1) * own_s, h * targets : (h + 1) * targets]
    weight = weight * (1.0 / (CHANNELS * 9.0**LAYERS))
    wide = (weight[:, None, :] * keep[:, :targets][None]).reshape(own_s * groups, targets)
    wexp[...] = jnp.dot(split_rows(wide), spread[...], preferred_element_type=jnp.float32)
    pred[...] = columns.T

    even = mask[4] % 2 == 0
    early = mask[4] < 2
    for m in range(own_s):
        sums = [[None] * PACK for _ in range(CHANNELS)]
        for g in range(groups):
            w = wexp[pl.ds(m * groups + g, SUB, stride=0), :]
            for channel in range(CHANNELS):
                for k in range(PACK):
                    value = w * unit[g, channel, k, m]
                    sums[channel][k] = value if g == 0 else sums[channel][k] + value
        for channel in range(CHANNELS):
            low = fold(sums[channel][0], sums[channel][1], even, SIDE)
            high = fold(sums[channel][2], sums[channel][3], even, SIDE)
            flat[channel, m] = fold(low, high, early, 2 * SIDE)
    residual = -own_onehot[:own_t, :CLASSES]
    for h in range(per):
        residual = residual + jnp.dot(
            pred[pl.ds(h * targets + ti * own_t, own_t), :], dual_rows(h),
            precision=HIGH, preferred_element_type=jnp.float32,
        )
    residual_ref[...] = residual
    for channel in range(CHANNELS):
        for s in range(SUB):
            grad_ref[channel, s] = flat[channel, :, s, :]


def hand_over(residual_ref, grad_ref, residual_out, grad_out):
    residual_out[...] = residual_ref[...]
    grad_out[...] = grad_ref[...]


def shards(nt, ns, target_pool, target_index, target_labels, dual_weights, support_images):
    own_t = target_index.shape[0]
    own_s = support_images.shape[0]
    groups_own = own_t // PACK
    groups = nt * groups_own
    chips = nt // 2
    ndev = nt * ns
    per = sharing(nt * own_t, own_s)
    f32 = jnp.float32
    vmem = pl.BlockSpec(memory_space=pltpu.VMEM)
    hbm = pl.BlockSpec(memory_space=pltpu.HBM)
    dma = pltpu.SemaphoreType.DMA
    tile = (SUB, LANES)
    pool = target_pool.reshape(-1, SUB, CHANNELS, SUB, LANES).transpose(2, 0, 3, 1, 4)
    support = support_images.reshape(own_s, CHANNELS, SUB, LANES).transpose(1, 2, 0, 3)
    residual, grad = pl.pallas_call(
        functools.partial(kernel, nt, ns, own_t, own_s),
        out_shape=(
            jax.ShapeDtypeStruct((own_t, CLASSES), f32),
            jax.ShapeDtypeStruct((CHANNELS, SUB, own_s, LANES), f32),
        ),
        in_specs=[hbm] * 5,
        out_specs=(vmem, vmem),
        scratch_shapes=[
            pltpu.SMEM((own_t,), jnp.int32),
            pltpu.SMEM((own_t,), jnp.int32),
            *[pltpu.VMEM(pool.shape[1:], f32)] * CHANNELS,
            pltpu.VMEM(support.shape, f32),
            pltpu.VMEM((nt, groups_own, CHANNELS * PACK) + tile, f32),
            pltpu.VMEM((ns,) + dual_weights.shape, f32),
            pltpu.VMEM((nt, 1, LANES), jnp.int32),
            pltpu.VMEM((ndev, own_s // per, per * nt * own_t), f32),
            pltpu.VMEM((2 * LANES, LANES), jnp.bfloat16),
            pltpu.VMEM((3 * LANES, per * nt * own_t), jnp.bfloat16),
            pltpu.VMEM((3 * nt * own_t, LANES), jnp.bfloat16),
            pltpu.VMEM((groups, per * nt * own_t), f32),
            pltpu.VMEM((CHANNELS, PACK, own_s) + tile, f32),
            pltpu.VMEM((LAYERS, 2, PACK, own_s) + tile, f32),
            pltpu.VMEM((LAYERS, PACK, own_s) + tile, f32),
            pltpu.VMEM((max(chips - 1, 1), 2, LAYERS - 1, 2, PACK) + tile, f32),
            pltpu.VMEM((2, PACK, own_s) + tile, f32),
            pltpu.VMEM((2, LAYERS, PACK, own_s) + tile, f32),
            pltpu.VMEM((groups, LAYERS, PACK, own_s) + tile, f32),
            pltpu.VMEM((groups, LAYERS, PACK, own_s) + tile, f32),
            pltpu.VMEM((groups, CHANNELS, PACK, own_s) + tile, f32),
            pltpu.VMEM((own_s, groups, LANES), f32),
            pltpu.VMEM((own_s * groups, LANES), f32),
            pltpu.VMEM((per * nt * own_t, ns * dual_weights.shape[0] // per), f32),
            pltpu.VMEM((CHANNELS, own_s) + tile, f32),
            dma((4 + CHANNELS,)),
            dma,
            dma((chips, groups_own)),
            dma,
            dma,
            dma,
            dma((chips, groups_own)),
            dma,
            dma,
            dma,
            dma,
            dma,
            dma,
        ],
        compiler_params=pltpu.CompilerParams(
            collective_id=0, has_side_effects=True, vmem_limit_bytes=44 * 2**20
        ),
    )(*[
        pltpu.with_memory_space_constraint(v, pltpu.HBM)
        for v in (target_index, target_labels, pool, dual_weights, support)
    ])
    residual, grad = pl.pallas_call(
        hand_over,
        out_shape=(
            jax.ShapeDtypeStruct(residual.shape, f32),
            jax.ShapeDtypeStruct(grad.shape, f32),
        ),
        in_specs=[vmem, vmem],
        out_specs=(vmem, vmem),
        compiler_params=pltpu.CompilerParams(vmem_limit_bytes=2**20),
    )(residual, grad)
    return (residual, grad.transpose(2, 0, 1, 3).reshape(support_images.shape))


def solution(mesh):
    in_specs = (
        P("tgt", None, None),
        P("tgt"),
        P("tgt"),
        P("sup", None),
        P(("sup", "tgt"), None, None),
    )
    out_specs = (P("tgt", None), P(("sup", "tgt"), None, None))
    body = functools.partial(shards, mesh.shape["tgt"], mesh.shape["sup"])
    return jax.shard_map(body, mesh=mesh, in_specs=in_specs, out_specs=out_specs, check_vma=False)
```
